256 devices in a mesh: grp: 4 (over z_hi), col: 16 (over y, z_lo, core), lay: 4 (over x).
Axes of the slice: x: 4, y: 4, z: 8 (z_hi: 4, z_lo: 2; z = z_hi * 2 + z_lo), core: 2. Of those that a mesh axis runs over, the one named last changes fastest.
Arguments:
- salinity: float32 [16, 1024, 2048], P('lay', ('grp', 'col')), may hold values from 0.3 to 4.2
- zone_ids: int32 [16, 1024, 2048], P('lay', ('grp', 'col')), may hold values from 0 to 7
- flow_speed: float32 [16, 1024, 2048], P('lay', ('grp', 'col')), may hold values from 0.5 to 4
- fixed_cells: int32 [16, 1024, 2048], P('lay', ('grp', 'col')), may hold values 0 or 1
- dispersivity: float32 [2, 8], replicated, may hold values from 50 to 1000
Outputs:
- salinity_next: float32 [16, 1024, 2048], P('lay', 'grp', 'col')
The draws below stay inside these ranges and needn't reach their ends.
All inputs are finite; a program needn't handle non-finite values. No bound on the sum of `fixed_cells` on one device may be relied on, other than what follows from the above.
Results may differ from the reference program's by a relative error of at most 0.00005.
Values sent between devices are 32-bit elements; how exact they have to be, the bound alone decides.
A program may use at most 128 MiB of HBM per device.

```python
import math
import jax
import jax.numpy as jnp
from jax import lax

NX = 2048
ZONES = 8
NZ = 16
NY = 1024
N_GRP = 4


def draw_salinity(key, part):
    level_key, cell_key = jax.random.split(jax.random.fold_in(key, 17))
    bands = 2 * N_GRP
    levels = jax.random.uniform(level_key, (bands,), jnp.float32, 0.5, 3.0)
    band_of_row = jnp.arange(NY, dtype=jnp.int32) * bands // NY
    row_levels = levels[band_of_row]
    factor = jax.random.uniform(cell_key, (NZ, NY, NX), jnp.float32, 0.8, 1.2)
    return (row_levels[None, :, None] * factor).astype(jnp.float32)


def plant(entries, rng, least, top_value):
    longest = entries.shape.index(max(entries.shape))
    spots = []
    for shift in (0, 1):
        where = [jax.random.randint(jax.random.fold_in(rng, axis), (), 0, length) for axis, length in enumerate(entries.shape)]
        where[longest] = (where[longest] + shift) % entries.shape[longest]
        spots.append(tuple(where))
    return entries.at[spots[0]].set(least).at[spots[1]].set(top_value)


def level_of(rng, extent, cuts, low, largest):
    loudness = 1.0
    for axis_at, parts in cuts:
        steps = jax.random.uniform(jax.random.fold_in(jax.random.fold_in(rng, 6), axis_at), (parts,), jnp.float32, low / len(cuts), largest / len(cuts))
        loudness = loudness * jnp.repeat(jnp.exp(steps), extent[axis_at] // parts).reshape((-1,) + (1,) * (len(extent) - 1 - axis_at))
    return loudness


def setup_inputs(seed: int = 0) -> dict:
    arg_keys = jax.random.split(jax.random.key(seed), 6)
    return {
        "salinity": draw_salinity(jax.random.fold_in(arg_keys[5], 71), 0),
        "zone_ids": plant(jax.random.randint(arg_keys[1], (NZ, NY, NX), 0, ZONES), jax.random.fold_in(arg_keys[1], 1), 0, ZONES - 1).astype(jnp.int32),
        "flow_speed": jnp.clip(jnp.exp(math.log(4.0) - 2.0794415 * jax.random.uniform(arg_keys[2], (NZ, NY, NX), jnp.float32) ** level_of(arg_keys[2], (NZ, NY, NX), ((0, 4), (1, 64)), -0.2, 0.2)), 0.5, 4.0),
        "fixed_cells": plant((jax.random.randint(arg_keys[3], (NZ, NY, NX), 0, 1024) < 1).astype(jnp.int32), jax.random.fold_in(arg_keys[3], 1), 0, 1),
        "dispersivity": jnp.clip(jnp.exp(jax.random.uniform(arg_keys[4], (2, ZONES), jnp.float32, math.log(50.0), math.log(1000.0))), 50.0, 1000.0),
    }


def shifted(values, stride, line_axis, filler, heading):
    line_axis = line_axis % values.ndim
    length = values.shape[line_axis]
    edge_shape = list(values.shape)
    edge_shape[line_axis] = length
    padding = jnp.full(tuple(edge_shape), filler, values.dtype)
    padded = jnp.concatenate([padding, values, padding], axis=line_axis)
    return lax.dynamic_slice_in_dim(padded, length + heading * stride, length, axis=line_axis)


def reduce_lines(below_coef, middle, above_coef, right_side, line_axis):
    length = middle.shape[line_axis]
    levels = max(1, (length - 1).bit_length())

    def one_level(_, carry):
        below_now, middle_now, above_now, right_now, stride = carry
        weight_below = -below_now / shifted(middle_now, stride, line_axis, 1.0, -1)
        weight_above = -above_now / shifted(middle_now, stride, line_axis, 1.0, 1)
        below_next = weight_below * shifted(below_now, stride, line_axis, 0.0, -1)
        above_next = weight_above * shifted(above_now, stride, line_axis, 0.0, 1)
        middle_next = middle_now + weight_below * shifted(above_now, stride, line_axis, 0.0, -1) + weight_above * shifted(below_now, stride, line_axis, 0.0, 1)
        right_next = right_now + weight_below * shifted(right_now, stride, line_axis, 0.0, -1) + weight_above * shifted(right_now, stride, line_axis, 0.0, 1)
        return (below_next, middle_next, above_next, right_next, stride * 2)

    result = lax.fori_loop(0, levels, one_level, (below_coef, middle, above_coef, right_side, jnp.int32(1)))
    return result[3] / result[1]


def line_solve(coupling, field, line_axis):
    return reduce_lines(-coupling, 1.0 + 2.0 * coupling, -coupling, field, line_axis - field.ndim)


def couplings(zone_ids, flow_speed, fixed_cells, dispersivity):
    opened = 1.0 - fixed_cells.astype(jnp.float32)
    longit = jnp.zeros(flow_speed.shape, jnp.float32)
    transv = jnp.zeros(flow_speed.shape, jnp.float32)
    for number in range(dispersivity.shape[1]):
        matched = zone_ids == number
        longit = jnp.where(matched, dispersivity[0, number], longit)
        transv = jnp.where(matched, dispersivity[1, number], transv)
    return opened * longit * flow_speed, opened * transv * flow_speed


def reference(salinity, zone_ids, flow_speed, fixed_cells, dispersivity):
    long_coupling, trans_coupling = couplings(zone_ids, flow_speed, fixed_cells, dispersivity)
    first = line_solve(long_coupling, salinity, 2)
    second = line_solve(trans_coupling, first, 1)
    return line_solve(trans_coupling, second, 0)
```

```python
import jax
import jax.numpy as jnp
from jax import lax
from jax.experimental import pallas as pl
from jax.experimental.pallas import tpu as pltpu
from jax.sharding import PartitionSpec as P

NCOL = 16
NGRP = 4
NLAY = 4
L = 4
RB = 16
LINES = L * RB
LANES = 128
STEP = 16
ROWS = NCOL * RB
ZCH = 4
ZR = ROWS // ZCH
FCH = 2
FL = L // FCH
MESH = pl.DeviceIdType.MESH
F32 = jnp.float32


def butterfly(parts, lane):
    parts = list(parts)
    for m in range(4):
        step = 1 << m
        high = (lane & step) != 0
        for i in range(16):
            if i & step:
                continue
            a, b = parts[i], parts[i + step]
            parts[i] = jnp.where(high, pltpu.roll(b, step, 1), a)
            parts[i + step] = jnp.where(high, b, pltpu.roll(a, LANES - step, 1))
    return parts


def pick(zone, table):
    for m in range(3):
        bit = (zone & (1 << m)) != 0
        table = [jnp.where(bit, table[i + 1], table[i]) for i in range(0, len(table), 2)]
    return table[0]


def kernel(
    sal_hbm, zone_hbm, flow_hbm, fixed_hbm, disp_ref, out_hbm,
    sal, zone, flow, fixed,
    long_nat, st, ft, ys, yf,
    us, uf, up, uq, ur,
    yd, yfd, yp, yw, yr, lev_a, lev_c, lev_i, tmp,
    gcoef, gval,
    sec, wu, pu, wd, pd, eu_in, ed_in, eu_out, ed_out, qu_in, qd_in, qu_out, qd_out, res,
    in_sem, s_send, s_recv, f_send, f_recv, gc_send, gc_recv, gv_send, gv_recv,
    e_send, e_recv, q_send, q_recv, out_sem,
):
    grp = lax.axis_index("grp")
    col = lax.axis_index("col")
    lay = lax.axis_index("lay")

    loads = [
        pltpu.make_async_copy(zone_hbm, zone, in_sem.at[0]),
        pltpu.make_async_copy(flow_hbm, flow, in_sem.at[1]),
        pltpu.make_async_copy(fixed_hbm, fixed, in_sem.at[2]),
        pltpu.make_async_copy(sal_hbm, sal, in_sem.at[3]),
    ]
    for copy in loads:
        copy.start()

    barrier = pltpu.get_barrier_semaphore()

    def greet_col(o, carry):
        pl.semaphore_signal(barrier, inc=1, device_id={"col": (col + o) % NCOL}, device_id_type=MESH)
        return carry

    lax.fori_loop(1, NCOL, greet_col, 0)
    for o in range(1, NGRP):
        pl.semaphore_signal(barrier, inc=1, device_id={"grp": (grp + o) % NGRP}, device_id_type=MESH)
    for o in (1, NLAY - 1):
        pl.semaphore_signal(barrier, inc=1, device_id={"lay": (lay + o) % NLAY}, device_id_type=MESH)

    lane = lax.broadcasted_iota(jnp.int32, (8, LANES), 1)

    for copy in loads[:3]:
        copy.wait()
    table_long = [disp_ref[0, i] for i in range(8)]
    table_trans = [disp_ref[1, i] for i in range(8)]

    def couple(z, carry):
        for half in range(2):
            rows = pl.ds(8 * half, 8)
            for b in range(NCOL):
                cols = pl.ds(LANES * b, LANES)
                ids = zone[z, rows, cols]
                speed = flow[z, rows, cols]
                opened = 1.0 - fixed[z, rows, cols].astype(F32)
                st[b, z, rows, :] = opened * pick(ids, table_trans) * speed
                long_nat[b, z, rows, :] = opened * pick(ids, table_long) * speed
        return carry

    lax.fori_loop(0, L, couple, 0)

    pl.semaphore_wait(barrier, NCOL - 1 + NGRP - 1 + 2)

    def s_copy(dest, source):
        return pltpu.make_async_remote_copy(
            src_ref=st.at[dest],
            dst_ref=ys.at[:, pl.ds(source * RB, RB), :],
            send_sem=s_send.at[dest],
            recv_sem=s_recv.at[source],
            device_id={"col": dest},
            device_id_type=MESH,
        )

    def s_start(o, carry):
        s_copy((col + o) % NCOL, col).start()
        return carry

    lax.fori_loop(1, NCOL, s_start, 0)
    ys[:, pl.ds(col * RB, RB), :] = st[col]

    loads[3].wait()

    def spread(z, carry):
        for half in range(2):
            rows = pl.ds(8 * half, 8)
            line = pl.ds(pl.multiple_of(z * RB + 8 * half, 8), 8)
            s_parts = butterfly([long_nat[b, z, rows, :] for b in range(NCOL)], lane)
            for j in range(STEP):
                us[j, line, :] = s_parts[j]
            f_parts = butterfly([sal[z, rows, pl.ds(LANES * b, LANES)] for b in range(NCOL)], lane)
            for j in range(STEP):
                uf[j, line, :] = f_parts[j]
        return carry

    lax.fori_loop(0, L, spread, 0)

    whole = (LINES, LANES)
    e = jnp.ones(whole, F32)
    r = jnp.ones(whole, F32)
    q = jnp.zeros(whole, F32)
    alpha = jnp.zeros(whole, F32)
    eb = jnp.ones(whole, F32)
    for j in range(1, STEP):
        s = us[j]
        f = uf[j]
        se = s * e
        w = 1.0 / (1.0 + s + se)
        p = s * w
        e = (1.0 + se) * w
        q = f * w + p * q
        r_now = r * p
        alpha = alpha + r * q
        eb = eb - r * r_now
        r = r_now
        up[j] = p
        uq[j] = q
        ur[j] = r

    lanes = lax.broadcasted_iota(jnp.int32, whole, 1)
    sub = lanes // 16
    low = lanes % 16
    first_block = lanes == 0
    last_block = lanes == LANES - 1

    def before(v, d):
        if d >= 8:
            return pltpu.roll(v, d // 8, 1)
        return jnp.where(sub >= d, pltpu.roll(v, 16 * d, 1), pltpu.roll(v, 16 * d + 1, 1))

    def after(v, d):
        if d >= 8:
            return pltpu.roll(v, LANES - d // 8, 1)
        return jnp.where(
            sub < 8 - d, pltpu.roll(v, LANES - 16 * d, 1), pltpu.roll(v, LANES - 16 * d - 1, 1)
        )

    s = us[0]
    ep_left = jnp.where(first_block, 1.0, before(e, 1))
    q_left = jnp.where(first_block, 0.0, before(q, 1))
    r_left = jnp.where(first_block, 0.0, before(r, 1))
    inv = 1.0 / (1.0 + s * (eb + ep_left))
    a = s * r_left * inv
    c = jnp.where(last_block, 0.0, s * r * inv)
    f = (uf[0] + s * (q_left + alpha)) * inv
    for m in range(7):
        d = 1 << m
        inv = 1.0 / (1.0 - a * before(c, d) - c * after(a, d))
        f = (f + a * before(f, d) + c * after(f, d)) * inv
        if m < 6:
            a, c = a * before(a, d) * inv, c * after(c, d) * inv
    uf[0] = f
    x = jnp.where(last_block, 0.0, after(f, 1))
    for j in range(STEP - 1, 0, -1):
        x = uq[j] + ur[j] * f + up[j] * x
        uf[j] = x

    def f_copy(chunk, dest, source):
        return pltpu.make_async_remote_copy(
            src_ref=ft.at[dest, pl.ds(chunk * FL, FL)],
            dst_ref=yf.at[pl.ds(chunk * FL, FL), pl.ds(source * RB, RB), :],
            send_sem=f_send.at[chunk, dest],
            recv_sem=f_recv.at[chunk, source],
            device_id={"col": dest},
            device_id_type=MESH,
        )

    for chunk in range(FCH):

        def gather(z, carry):
            for half in range(2):
                rows = pl.ds(8 * half, 8)
                line = pl.ds(pl.multiple_of(z * RB + 8 * half, 8), 8)
                parts = butterfly([uf[j, line, :] for j in range(STEP)], lane)
                for b in range(NCOL):
                    ft[b, z, rows, :] = parts[b]
            return carry

        lax.fori_loop(chunk * FL, (chunk + 1) * FL, gather, 0)

        def f_start(o, carry):
            f_copy(chunk, (col + o) % NCOL, col).start()
            return carry

        lax.fori_loop(1, NCOL, f_start, 0)
        layers = pl.ds(chunk * FL, FL)
        yf[layers, pl.ds(col * RB, RB), :] = ft[col, layers]

    def s_wait(o, carry):
        s_copy(col, (col + NCOL - o) % NCOL).wait_recv()
        return carry

    lax.fori_loop(1, NCOL, s_wait, 0)

    def rows_of(z, h, j):
        return (z, pl.ds(128 * h + j, 8, stride=STEP), slice(None))

    for z in range(L):
        for h in range(2):
            for j in range(STEP):
                yd[j, pl.ds(16 * z + 8 * h, 8), :] = ys[rows_of(z, h, j)]

    e = jnp.ones(whole, F32)
    r = jnp.ones(whole, F32)
    eb = jnp.ones(whole, F32)
    for j in range(1, STEP):
        s = yd[j]
        se = s * e
        w = 1.0 / (1.0 + s + se)
        p = s * w
        e = (1.0 + se) * w
        r_now = r * p
        eb = eb - r * r_now
        r = r_now
        yw[j] = w
        yp[j] = p
        yr[j] = r
    block = lax.broadcasted_iota(jnp.int32, whole, 0) % RB

    def above(v, d, edge):
        return jnp.where(block >= d, pltpu.roll(v, d, 0), edge)

    def below(v, d, edge):
        return jnp.where(block < RB - d, pltpu.roll(v, LINES - d, 0), edge)

    s = yd[0]
    inv = 1.0 / (1.0 + s * (eb + above(e, 1, 1.0)))
    a = s * above(r, 1, 1.0) * inv
    c = s * r * inv
    yw[0] = inv
    for m in range(4):
        d = 1 << m
        inv = 1.0 / (1.0 - a * above(c, d, 0.0) - c * below(a, d, 0.0))
        lev_a[m] = a * inv
        lev_c[m] = c * inv
        lev_i[m] = inv
        a, c = a * above(a, d, 1.0) * inv, c * below(c, d, 1.0) * inv
    lev_a[4] = a
    lev_c[4] = c
    top = pl.ds(0, L, stride=RB)
    bottom = pl.ds(RB - 1, L, stride=RB)
    tmp[0] = r * a
    tmp[1] = (1.0 - e) + r * c
    gcoef[grp, 0] = lev_a[4, top, :]
    gcoef[grp, 1] = lev_c[4, top, :]
    gcoef[grp, 2] = tmp[0, bottom, :]
    gcoef[grp, 3] = tmp[1, bottom, :]

    def g_copy(buf, send, recv, dest, source):
        return pltpu.make_async_remote_copy(
            src_ref=buf.at[source],
            dst_ref=buf.at[source],
            send_sem=send.at[dest],
            recv_sem=recv.at[source],
            device_id={"grp": dest},
            device_id_type=MESH,
        )

    for o in range(1, NGRP):
        g_copy(gcoef, gc_send, gc_recv, (grp + o) % NGRP, grp).start()

    def e_copy(way, c, dest):
        rows = pl.ds(pl.multiple_of(c * ZR, ZR), ZR)
        src, dst = ((eu_out, eu_in), (ed_out, ed_in))[way]
        return pltpu.make_async_remote_copy(
            src_ref=src.at[rows],
            dst_ref=dst.at[rows],
            send_sem=e_send.at[way, c],
            recv_sem=e_recv.at[way, c],
            device_id={"lay": dest},
            device_id_type=MESH,
        )

    def q_copy(way, c, dest):
        rows = pl.ds(pl.multiple_of(c * ZR, ZR), ZR)
        src, dst = ((qu_out, qu_in), (qd_out, qd_in))[way]
        return pltpu.make_async_remote_copy(
            src_ref=src.at[rows],
            dst_ref=dst.at[rows],
            send_sem=q_send.at[way, c],
            recv_sem=q_recv.at[way, c],
            device_id={"lay": dest},
            device_id_type=MESH,
        )

    @pl.when(lay == 0)
    def _():
        eu_in[...] = jnp.ones((ROWS, LANES), F32)
        qu_in[...] = jnp.zeros((ROWS, LANES), F32)

    @pl.when(lay == NLAY - 1)
    def _():
        ed_in[...] = jnp.ones((ROWS, LANES), F32)
        qd_in[...] = jnp.zeros((ROWS, LANES), F32)

    def e_step(t, carry):
        for way in range(2):
            back = lay if way == 0 else NLAY - 1 - lay
            dest = jnp.minimum(lay + 1, NLAY - 1) if way == 0 else jnp.maximum(lay - 1, 0)
            c = t - back

            @pl.when((c >= 0) & (c < ZCH))
            def _():
                rows = pl.ds(pl.multiple_of(c * ZR, ZR), ZR)
                src, out, wr, pr = ((eu_in, eu_out, wu, pu), (ed_in, ed_out, wd, pd))[way]

                @pl.when(back > 0)
                def _():
                    e_copy(way, c, dest).wait_recv()

                e = src[rows, :]
                for i in range(L) if way == 0 else range(L - 1, -1, -1):
                    s = ys[i, rows, :]
                    se = s * e
                    w = 1.0 / (1.0 + s + se)
                    e = (1.0 + se) * w
                    wr[i, rows, :] = w
                    pr[i, rows, :] = s * w
                out[rows, :] = e

                @pl.when(back < NLAY - 1)
                def _():
                    e_copy(way, c, dest).start()

        return carry

    lax.fori_loop(0, ZCH + NLAY - 1, e_step, 0)

    for chunk in range(FCH):

        def f_wait(o, carry):
            f_copy(chunk, col, (col + NCOL - o) % NCOL).wait_recv()
            return carry

        lax.fori_loop(1, NCOL, f_wait, 0)
        for z in range(chunk * FL, (chunk + 1) * FL):
            for h in range(2):
                for j in range(STEP):
                    yfd[j, pl.ds(16 * z + 8 * h, 8), :] = yf[rows_of(z, h, j)]

    q = yfd[1] * yw[1]
    yfd[1] = q
    alpha = q
    for j in range(2, STEP):
        q = yfd[j] * yw[j] + yp[j] * q
        yfd[j] = q
        alpha = alpha + yr[j - 1] * q
    f = (yfd[0] + yd[0] * (above(q, 1, 0.0) + alpha)) * yw[0]
    for m in range(4):
        d = 1 << m
        f = f * lev_i[m] + lev_a[m] * above(f, d, 0.0) + lev_c[m] * below(f, d, 0.0)
    tmp[2] = f
    tmp[3] = q + yr[STEP - 1] * f
    gval[grp, 0] = tmp[2, top, :]
    gval[grp, 1] = tmp[3, bottom, :]
    for o in range(1, NGRP):
        g_copy(gval, gv_send, gv_recv, (grp + o) % NGRP, grp).start()
    for o in range(1, NGRP):
        g_copy(gcoef, gc_send, gc_recv, grp, (grp + NGRP - o) % NGRP).wait_recv()
    for o in range(1, NGRP):
        g_copy(gval, gv_send, gv_recv, grp, (grp + NGRP - o) % NGRP).wait_recv()

    be = [gcoef[g, 0] for g in range(NGRP)]
    ga = [gcoef[g, 1] for g in range(NGRP)]
    rr = [gcoef[g, 2] for g in range(NGRP)]
    pp = [gcoef[g, 3] for g in range(NGRP)]
    al = [gval[g, 0] for g in range(NGRP)]
    qq = [gval[g, 1] for g in range(NGRP)]
    pre_p, pre_q = [pp[0]], [qq[0]]
    for g in range(1, NGRP - 1):
        t = rr[g] / (1.0 - pre_p[-1] * be[g])
        pre_p, pre_q = (
            pre_p + [pp[g] + t * pre_p[-1] * ga[g]],
            pre_q + [qq[g] + t * (pre_q[-1] + pre_p[-1] * al[g])],
        )
    suf_p, suf_q = [be[NGRP - 1]], [al[NGRP - 1]]
    for g in range(NGRP - 2, 0, -1):
        t = ga[g] * suf_p[0] / (1.0 - pp[g] * suf_p[0])
        suf_p, suf_q = (
            [be[g] + t * rr[g]] + suf_p,
            [al[g] + ga[g] * suf_q[0] + t * (qq[g] + pp[g] * suf_q[0])] + suf_q,
        )
    left = jnp.zeros((L, LANES), F32)
    right = jnp.zeros((L, LANES), F32)
    for i in range(NGRP - 1):
        u = (pre_q[i] + pre_p[i] * suf_q[i]) / (1.0 - pre_p[i] * suf_p[i])
        v = suf_q[i] + suf_p[i] * u
        left = jnp.where(grp == i + 1, u, left)
        right = jnp.where(grp == i, v, right)

    def per_line(v):
        return jnp.concatenate([jnp.broadcast_to(v[z : z + 1], (RB, LANES)) for z in range(L)], 0)

    right = per_line(right)
    f = f + lev_a[4] * per_line(left) + lev_c[4] * right
    x = jnp.where(block == RB - 1, right, pltpu.roll(f, LINES - 1, 0))
    for j in range(STEP - 1, -1, -1):
        if j == 0:
            x = f
        else:
            x = yfd[j] + yr[j] * f + yp[j] * x
        for z in range(L):
            for h in range(2):
                m = 16 * z + 8 * h
                sec[rows_of(z, h, j)] = x[m : m + 8]

    def q_step(t, carry):
        for way in range(2):
            back = lay if way == 0 else NLAY - 1 - lay
            dest = jnp.minimum(lay + 1, NLAY - 1) if way == 0 else jnp.maximum(lay - 1, 0)
            c = t - back

            @pl.when((c >= 0) & (c < ZCH))
            def _():
                rows = pl.ds(pl.multiple_of(c * ZR, ZR), ZR)
                src, out, wr, pr = ((qu_in, qu_out, wu, pu), (qd_in, qd_out, wd, pd))[way]
                order = range(L) if way == 0 else range(L - 1, -1, -1)

                @pl.when(back > 0)
                def _():
                    q_copy(way, c, dest).wait_recv()

                q = src[rows, :]
                for i in order:
                    q = sec[i, rows, :] * wr[i, rows, :] + pr[i, rows, :] * q
                    if way == 0:
                        res[i, rows, :] = q
                out[rows, :] = q

                @pl.when(back < NLAY - 1)
                def _():
                    q_copy(way, c, dest).start()

        c = t - jnp.maximum(lay, NLAY - 1 - lay)

        @pl.when((c >= 0) & (c < ZCH))
        def _():
            rows = pl.ds(pl.multiple_of(c * ZR, ZR), ZR)
            ep = eu_out[rows, :]
            p = 1.0 - ep
            x = (res[L - 1, rows, :] + p * qd_in[rows, :]) / (ep + p * ed_in[rows, :])
            res[L - 1, rows, :] = x
            for i in range(L - 2, -1, -1):
                x = res[i, rows, :] + pu[i, rows, :] * x
                res[i, rows, :] = x
            pltpu.make_async_copy(res.at[:, rows, :], out_hbm.at[:, rows, :], out_sem.at[c]).start()

        return carry

    lax.fori_loop(0, ZCH + NLAY - 1, q_step, 0)

    def s_done(o, carry):
        s_copy((col + o) % NCOL, col).wait_send()
        for chunk in range(FCH):
            f_copy(chunk, (col + o) % NCOL, col).wait_send()
        return carry

    lax.fori_loop(1, NCOL, s_done, 0)
    for o in range(1, NGRP):
        g_copy(gcoef, gc_send, gc_recv, (grp + o) % NGRP, grp).wait_send()
        g_copy(gval, gv_send, gv_recv, (grp + o) % NGRP, grp).wait_send()
    for c in range(ZCH):

        @pl.when(lay < NLAY - 1)
        def _():
            e_copy(0, c, jnp.minimum(lay + 1, NLAY - 1)).wait_send()
            q_copy(0, c, jnp.minimum(lay + 1, NLAY - 1)).wait_send()

        @pl.when(lay > 0)
        def _():
            e_copy(1, c, jnp.maximum(lay - 1, 0)).wait_send()
            q_copy(1, c, jnp.maximum(lay - 1, 0)).wait_send()

        rows = pl.ds(c * ZR, ZR)
        pltpu.make_async_copy(res.at[:, rows, :], out_hbm.at[:, rows, :], out_sem.at[c]).wait()


def per_device(salinity, zone_ids, flow_speed, fixed_cells, dispersivity):
    hbm = pl.BlockSpec(memory_space=pl.ANY)
    nat = (L, RB, NCOL * LANES)
    slab = (L, ROWS, LANES)
    by_dest = (NCOL, L, RB, LANES)
    steps = (STEP, LINES, LANES)
    plane = (ROWS, LANES)

    def vm(shape, dtype=F32):
        return pltpu.VMEM(shape, dtype)

    dma = pltpu.SemaphoreType.DMA
    return pl.pallas_call(
        kernel,
        out_shape=jax.ShapeDtypeStruct(slab, F32),
        in_specs=[hbm, hbm, hbm, hbm, pl.BlockSpec(memory_space=pltpu.SMEM)],
        out_specs=hbm,
        scratch_shapes=[
            vm(nat), vm(nat, jnp.int32), vm(nat), vm(nat, jnp.int32),
            vm(by_dest), vm(by_dest), vm(by_dest), vm(slab), vm(slab),
            vm(steps), vm(steps), vm(steps), vm(steps), vm(steps),
            vm(steps), vm(steps), vm(steps), vm(steps), vm(steps),
            vm((5, LINES, LANES)), vm((5, LINES, LANES)), vm((4, LINES, LANES)), vm((4, LINES, LANES)),
            vm((NGRP, 4, L, LANES)), vm((NGRP, 2, L, LANES)),
            vm(slab), vm(slab), vm(slab), vm(slab), vm(slab),
            vm(plane), vm(plane), vm(plane), vm(plane), vm(plane), vm(plane), vm(plane), vm(plane),
            vm(slab),
            dma((4,)), dma((NCOL,)), dma((NCOL,)), dma((FCH, NCOL)), dma((FCH, NCOL)),
            dma((NGRP,)), dma((NGRP,)), dma((NGRP,)), dma((NGRP,)),
            dma((2, ZCH)), dma((2, ZCH)), dma((2, ZCH)), dma((2, ZCH)), dma((ZCH,)),
        ],
        compiler_params=pltpu.CompilerParams(
            collective_id=0, has_side_effects=True, vmem_limit_bytes=56 * 1024 * 1024
        ),
        name="lod_step",
    )(salinity, zone_ids, flow_speed, fixed_cells, dispersivity)


def solution(mesh):
    placed = P("lay", ("grp", "col"), None)
    return jax.shard_map(
        per_device,
        mesh=mesh,
        in_specs=(placed, placed, placed, placed, P()),
        out_specs=P("lay", "grp", "col"),
        check_vma=False,
    )
```

```python
import jax
import jax.numpy as jnp
from jax import lax
from jax.experimental import pallas as pl
from jax.experimental.pallas import tpu as pltpu
from jax.sharding import PartitionSpec as P

NCOL = 16
NGRP = 4
NLAY = 4
L = 4
RB = 16
LINES = L * RB
LANES = 128
STEP = 16
ROWS = NCOL * RB
ZCH = 4
ZR = ROWS // ZCH
QCH = 2
QR = ROWS // QCH
FCH = 2
FL = L // FCH
MESH = pl.DeviceIdType.MESH
F32 = jnp.float32


def butterfly(parts, lane):
    parts = list(parts)
    for m in range(4):
        step = 1 << m
        high = (lane & step) != 0
        for i in range(16):
            if i & step:
                continue
            a, b = parts[i], parts[i + step]
            parts[i] = jnp.where(high, pltpu.roll(b, step, 1), a)
            parts[i + step] = jnp.where(high, b, pltpu.roll(a, LANES - step, 1))
    return parts


def pick(zone, table):
    for m in range(3):
        bit = (zone & (1 << m)) != 0
        table = [jnp.where(bit, table[i + 1], table[i]) for i in range(0, len(table), 2)]
    return table[0]


def kernel(
    sal_hbm, zone_hbm, flow_hbm, fixed_hbm, disp_ref, out_hbm,
    sal, zone, flow, fixed,
    long_nat, st, ft, ys, yf,
    us, uf, up, uq, ur,
    yd, yfd, yp, yw, yr, lev_a, lev_c, lev_i, tmp,
    gcoef, gval,
    sec, wu, pu, wd, pd, eu_in, ed_in, eu_out, ed_out, ru, rd, r_in, qu_out, qd_out, q_in, res,
    in_sem, s_send, s_recv, f_send, f_recv, gc_send, gc_recv, gv_send, gv_recv,
    e_send, e_recv, r_send, r_recv, q_send, q_recv, out_sem,
):
    grp = lax.axis_index("grp")
    col = lax.axis_index("col")
    lay = lax.axis_index("lay")

    def s_copy(dest, source):
        return pltpu.make_async_remote_copy(
            src_ref=st.at[dest],
            dst_ref=ys.at[:, pl.ds(source * RB, RB), :],
            send_sem=s_send.at[dest],
            recv_sem=s_recv.at[source],
            device_id={"col": dest},
            device_id_type=MESH,
        )

    def f_copy(chunk, dest, source):
        return pltpu.make_async_remote_copy(
            src_ref=ft.at[dest, pl.ds(chunk * FL, FL)],
            dst_ref=yf.at[pl.ds(chunk * FL, FL), pl.ds(source * RB, RB), :],
            send_sem=f_send.at[chunk, dest],
            recv_sem=f_recv.at[chunk, source],
            device_id={"col": dest},
            device_id_type=MESH,
        )

    def g_copy(buf, send, recv, dest, source):
        return pltpu.make_async_remote_copy(
            src_ref=buf.at[source],
            dst_ref=buf.at[source],
            send_sem=send.at[dest],
            recv_sem=recv.at[source],
            device_id={"grp": dest},
            device_id_type=MESH,
        )

    def e_copy(way, c, dest):
        rows = pl.ds(pl.multiple_of(c * ZR, ZR), ZR)
        src, dst = ((eu_out, eu_in), (ed_out, ed_in))[way]
        return pltpu.make_async_remote_copy(
            src_ref=src.at[rows],
            dst_ref=dst.at[rows],
            send_sem=e_send.at[way, c],
            recv_sem=e_recv.at[way, c],
            device_id={"lay": dest},
            device_id_type=MESH,
        )

    def r_copy(way, dest, source):
        return pltpu.make_async_remote_copy(
            src_ref=(ru, rd)[way],
            dst_ref=r_in.at[source],
            send_sem=r_send.at[dest],
            recv_sem=r_recv.at[source],
            device_id={"lay": dest},
            device_id_type=MESH,
        )

    def q_copy(way, c, dest, source):
        rows = pl.ds(pl.multiple_of(c * QR, QR), QR)
        return pltpu.make_async_remote_copy(
            src_ref=(qu_out, qd_out)[way].at[rows],
            dst_ref=q_in.at[source, rows],
            send_sem=q_send.at[c, dest],
            recv_sem=q_recv.at[c, source],
            device_id={"lay": dest},
            device_id_type=MESH,
        )

    def out_copy(c):
        rows = pl.ds(pl.multiple_of(c * QR, QR), QR)
        return pltpu.make_async_copy(res.at[:, rows, :], out_hbm.at[:, rows, :], out_sem.at[c])

    def ahead(way, k):
        return range(k + 1, NLAY) if way == 0 else range(k - 1, -1, -1)

    def e_stage(k):
        for way in range(2):

            @pl.when(lay == (k if way == 0 else NLAY - 1 - k))
            def _():
                me = k if way == 0 else NLAY - 1 - k
                src, out, wr, pr, prod = ((eu_in, eu_out, wu, pu, ru), (ed_in, ed_out, wd, pd, rd))[way]

                def step(c, carry):
                    rows = pl.ds(pl.multiple_of(c * ZR, ZR), ZR)
                    if k > 0:
                        e_copy(way, c, me).wait_recv()
                        e = src[rows, :]
                    else:
                        e = jnp.ones((ZR, LANES), F32)
                    total = None
                    for i in range(L) if way == 0 else range(L - 1, -1, -1):
                        s = ys[i, rows, :]
                        se = s * e
                        w = 1.0 / (1.0 + s + se)
                        e = (1.0 + se) * w
                        p = s * w
                        wr[i, rows, :] = w
                        pr[i, rows, :] = p
                        total = p if total is None else total * p
                    out[rows, :] = e
                    prod[rows, :] = total
                    if k < NLAY - 1:
                        e_copy(way, c, ahead(way, me)[0]).start()
                    return carry

                lax.fori_loop(0, ZCH, step, 0)
                if 0 < k < NLAY - 1:
                    for dest in ahead(way, me):
                        r_copy(way, dest, me).start()

    loads = [
        pltpu.make_async_copy(zone_hbm, zone, in_sem.at[0]),
        pltpu.make_async_copy(flow_hbm, flow, in_sem.at[1]),
        pltpu.make_async_copy(fixed_hbm, fixed, in_sem.at[2]),
        pltpu.make_async_copy(sal_hbm, sal, in_sem.at[3]),
    ]
    for copy in loads:
        copy.start()

    barrier = pltpu.get_barrier_semaphore()

    def greet_col(o, carry):
        pl.semaphore_signal(barrier, inc=1, device_id={"col": (col + o) % NCOL}, device_id_type=MESH)
        return carry

    lax.fori_loop(1, NCOL, greet_col, 0)
    for o in range(1, NGRP):
        pl.semaphore_signal(barrier, inc=1, device_id={"grp": (grp + o) % NGRP}, device_id_type=MESH)
    for o in (1, NLAY - 1):
        pl.semaphore_signal(barrier, inc=1, device_id={"lay": (lay + o) % NLAY}, device_id_type=MESH)

    lane = lax.broadcasted_iota(jnp.int32, (8, LANES), 1)

    for copy in loads[:3]:
        copy.wait()
    table_long = [disp_ref[0, i] for i in range(8)]
    table_trans = [disp_ref[1, i] for i in range(8)]

    def couple(z, carry):
        for half in range(2):
            rows = pl.ds(8 * half, 8)
            for b in range(NCOL):
                cols = pl.ds(LANES * b, LANES)
                ids = zone[z, rows, cols]
                speed = flow[z, rows, cols]
                opened = 1.0 - fixed[z, rows, cols].astype(F32)
                st[b, z, rows, :] = opened * pick(ids, table_trans) * speed
                long_nat[b, z, rows, :] = opened * pick(ids, table_long) * speed
        return carry

    lax.fori_loop(0, L, couple, 0)

    pl.semaphore_wait(barrier, NCOL - 1 + NGRP - 1 + 2)

    def s_start(o, carry):
        s_copy((col + o) % NCOL, col).start()
        return carry

    lax.fori_loop(1, NCOL, s_start, 0)
    ys[:, pl.ds(col * RB, RB), :] = st[col]

    loads[3].wait()

    def spread(z, carry):
        for half in range(2):
            rows = pl.ds(8 * half, 8)
            line = pl.ds(pl.multiple_of(z * RB + 8 * half, 8), 8)
            s_parts = butterfly([long_nat[b, z, rows, :] for b in range(NCOL)], lane)
            for j in range(STEP):
                us[j, line, :] = s_parts[j]
            f_parts = butterfly([sal[z, rows, pl.ds(LANES * b, LANES)] for b in range(NCOL)], lane)
            for j in range(STEP):
                uf[j, line, :] = f_parts[j]
        return carry

    lax.fori_loop(0, L, spread, 0)

    whole = (LINES, LANES)
    e = jnp.ones(whole, F32)
    r = jnp.ones(whole, F32)
    q = jnp.zeros(whole, F32)
    alpha = jnp.zeros(whole, F32)
    eb = jnp.ones(whole, F32)
    for j in range(1, STEP):
        s = us[j]
        f = uf[j]
        se = s * e
        w = 1.0 / (1.0 + s + se)
        p = s * w
        e = (1.0 + se) * w
        q = f * w + p * q
        r_now = r * p
        alpha = alpha + r * q
        eb = eb - r * r_now
        r = r_now
        up[j] = p
        uq[j] = q
        ur[j] = r

    lanes = lax.broadcasted_iota(jnp.int32, whole, 1)
    sub = lanes // 16
    low = lanes % 16
    first_block = lanes == 0
    last_block = lanes == LANES - 1

    def before(v, d):
        if d >= 8:
            return pltpu.roll(v, d // 8, 1)
        return jnp.where(sub >= d, pltpu.roll(v, 16 * d, 1), pltpu.roll(v, 16 * d + 1, 1))

    def after(v, d):
        if d >= 8:
            return pltpu.roll(v, LANES - d // 8, 1)
        return jnp.where(
            sub < 8 - d, pltpu.roll(v, LANES - 16 * d, 1), pltpu.roll(v, LANES - 16 * d - 1, 1)
        )

    s = us[0]
    ep_left = jnp.where(first_block, 1.0, before(e, 1))
    q_left = jnp.where(first_block, 0.0, before(q, 1))
    r_left = jnp.where(first_block, 0.0, before(r, 1))
    inv = 1.0 / (1.0 + s * (eb + ep_left))
    a = s * r_left * inv
    c = jnp.where(last_block, 0.0, s * r * inv)
    f = (uf[0] + s * (q_left + alpha)) * inv
    for m in range(7):
        d = 1 << m
        inv = 1.0 / (1.0 - a * before(c, d) - c * after(a, d))
        f = (f + a * before(f, d) + c * after(f, d)) * inv
        if m < 6:
            a, c = a * before(a, d) * inv, c * after(c, d) * inv

    uf[0] = f
    x = jnp.where(last_block, 0.0, after(f, 1))
    for j in range(STEP - 1, 0, -1):
        x = uq[j] + ur[j] * f + up[j] * x
        uf[j] = x

    for chunk in range(FCH):

        def gather(z, carry):
            for half in range(2):
                rows = pl.ds(8 * half, 8)
                line = pl.ds(pl.multiple_of(z * RB + 8 * half, 8), 8)
                parts = butterfly([uf[j, line, :] for j in range(STEP)], lane)
                for b in range(NCOL):
                    ft[b, z, rows, :] = parts[b]
            return carry

        lax.fori_loop(chunk * FL, (chunk + 1) * FL, gather, 0)

        def f_start(o, carry):
            f_copy(chunk, (col + o) % NCOL, col).start()
            return carry

        lax.fori_loop(1, NCOL, f_start, 0)
        layers = pl.ds(chunk * FL, FL)
        yf[layers, pl.ds(col * RB, RB), :] = ft[col, layers]

    def s_wait(o, carry):
        s_copy(col, (col + NCOL - o) % NCOL).wait_recv()
        return carry

    lax.fori_loop(1, NCOL, s_wait, 0)

    e_stage(0)

    def rows_of(z, h, j):
        return (z, pl.ds(128 * h + j, 8, stride=STEP), slice(None))

    for z in range(L):
        for h in range(2):
            for j in range(STEP):
                yd[j, pl.ds(16 * z + 8 * h, 8), :] = ys[rows_of(z, h, j)]

    e = jnp.ones(whole, F32)
    r = jnp.ones(whole, F32)
    eb = jnp.ones(whole, F32)
    for j in range(1, STEP):
        s = yd[j]
        se = s * e
        w = 1.0 / (1.0 + s + se)
        p = s * w
        e = (1.0 + se) * w
        r_now = r * p
        eb = eb - r * r_now
        r = r_now
        yw[j] = w
        yp[j] = p
        yr[j] = r
    block = lax.broadcasted_iota(jnp.int32, whole, 0) % RB

    def above(v, d, edge):
        return jnp.where(block >= d, pltpu.roll(v, d, 0), edge)

    def below(v, d, edge):
        return jnp.where(block < RB - d, pltpu.roll(v, LINES - d, 0), edge)

    s = yd[0]
    inv = 1.0 / (1.0 + s * (eb + above(e, 1, 1.0)))
    a = s * above(r, 1, 1.0) * inv
    c = s * r * inv
    yw[0] = inv
    for m in range(4):
        d = 1 << m
        inv = 1.0 / (1.0 - a * above(c, d, 0.0) - c * below(a, d, 0.0))
        lev_a[m] = a * inv
        lev_c[m] = c * inv
        lev_i[m] = inv
        a, c = a * above(a, d, 1.0) * inv, c * below(c, d, 1.0) * inv
    lev_a[4] = a
    lev_c[4] = c
    top = pl.ds(0, L, stride=RB)
    bottom = pl.ds(RB - 1, L, stride=RB)
    tmp[0] = r * a
    tmp[1] = (1.0 - e) + r * c
    gcoef[grp, 0] = lev_a[4, top, :]
    gcoef[grp, 1] = lev_c[4, top, :]
    gcoef[grp, 2] = tmp[0, bottom, :]
    gcoef[grp, 3] = tmp[1, bottom, :]

    for o in range(1, NGRP):
        g_copy(gcoef, gc_send, gc_recv, (grp + o) % NGRP, grp).start()

    e_stage(1)

    for chunk in range(FCH):

        def f_wait(o, carry):
            f_copy(chunk, col, (col + NCOL - o) % NCOL).wait_recv()
            return carry

        lax.fori_loop(1, NCOL, f_wait, 0)
        for z in range(chunk * FL, (chunk + 1) * FL):
            for h in range(2):
                for j in range(STEP):
                    yfd[j, pl.ds(16 * z + 8 * h, 8), :] = yf[rows_of(z, h, j)]

    q = yfd[1] * yw[1]
    yfd[1] = q
    alpha = q
    for j in range(2, STEP):
        q = yfd[j] * yw[j] + yp[j] * q
        yfd[j] = q
        alpha = alpha + yr[j - 1] * q
    f = (yfd[0] + yd[0] * (above(q, 1, 0.0) + alpha)) * yw[0]
    for m in range(4):
        d = 1 << m
        f = f * lev_i[m] + lev_a[m] * above(f, d, 0.0) + lev_c[m] * below(f, d, 0.0)
    tmp[2] = f
    tmp[3] = q + yr[STEP - 1] * f
    gval[grp, 0] = tmp[2, top, :]
    gval[grp, 1] = tmp[3, bottom, :]

    for o in range(1, NGRP):
        g_copy(gval, gv_send, gv_recv, (grp + o) % NGRP, grp).start()

    e_stage(2)
    e_stage(3)

    for o in range(1, NGRP):
        g_copy(gcoef, gc_send, gc_recv, grp, (grp + NGRP - o) % NGRP).wait_recv()
    for o in range(1, NGRP):
        g_copy(gval, gv_send, gv_recv, grp, (grp + NGRP - o) % NGRP).wait_recv()

    be = [gcoef[g, 0] for g in range(NGRP)]
    ga = [gcoef[g, 1] for g in range(NGRP)]
    rr = [gcoef[g, 2] for g in range(NGRP)]
    pp = [gcoef[g, 3] for g in range(NGRP)]
    al = [gval[g, 0] for g in range(NGRP)]
    qq = [gval[g, 1] for g in range(NGRP)]
    pre_p, pre_q = [pp[0]], [qq[0]]
    for g in range(1, NGRP - 1):
        t = rr[g] / (1.0 - pre_p[-1] * be[g])
        pre_p, pre_q = (
            pre_p + [pp[g] + t * pre_p[-1] * ga[g]],
            pre_q + [qq[g] + t * (pre_q[-1] + pre_p[-1] * al[g])],
        )
    suf_p, suf_q = [be[NGRP - 1]], [al[NGRP - 1]]
    for g in range(NGRP - 2, 0, -1):
        t = ga[g] * suf_p[0] / (1.0 - pp[g] * suf_p[0])
        suf_p, suf_q = (
            [be[g] + t * rr[g]] + suf_p,
            [al[g] + ga[g] * suf_q[0] + t * (qq[g] + pp[g] * suf_q[0])] + suf_q,
        )
    left = jnp.zeros((L, LANES), F32)
    right = jnp.zeros((L, LANES), F32)
    for i in range(NGRP - 1):
        u = (pre_q[i] + pre_p[i] * suf_q[i]) / (1.0 - pre_p[i] * suf_p[i])
        v = suf_q[i] + suf_p[i] * u
        left = jnp.where(grp == i + 1, u, left)
        right = jnp.where(grp == i, v, right)

    def per_line(v):
        return jnp.concatenate([jnp.broadcast_to(v[z : z + 1], (RB, LANES)) for z in range(L)], 0)

    right = per_line(right)
    f = f + lev_a[4] * per_line(left) + lev_c[4] * right
    x = jnp.where(block == RB - 1, right, pltpu.roll(f, LINES - 1, 0))
    for j in range(STEP - 1, -1, -1):
        if j == 0:
            x = f
        else:
            x = yfd[j] + yr[j] * f + yp[j] * x
        for z in range(L):
            for h in range(2):
                m = 16 * z + 8 * h
                sec[rows_of(z, h, j)] = x[m : m + 8]

    def q_local(c, carry):
        rows = pl.ds(pl.multiple_of(c * QR, QR), QR)
        for way in range(2):
            out, wr, pr = ((qu_out, wu, pu), (qd_out, wd, pd))[way]
            order = list(range(L) if way == 0 else range(L - 1, -1, -1))
            q = sec[order[0], rows, :] * wr[order[0], rows, :]
            for i in order[1:]:
                q = sec[i, rows, :] * wr[i, rows, :] + pr[i, rows, :] * q
            out[rows, :] = q
        for k in range(NLAY):

            @pl.when(lay == k)
            def _():
                for way in range(2):
                    for dest in reversed(ahead(way, k)):
                        q_copy(way, c, dest, k).start()

        return carry

    lax.fori_loop(0, QCH, q_local, 0)

    for k in range(NLAY):

        @pl.when(lay == k)
        def _():
            for source in (1, 2):
                if source != k:
                    r_copy(0, k, source).wait_recv()

            def finish(c, carry):
                rows = pl.ds(pl.multiple_of(c * QR, QR), QR)
                for source in range(NLAY):
                    if source != k:
                        q_copy(0, c, k, source).wait_recv()
                behind = []
                for way in range(2):
                    order = range(k) if way == 0 else range(NLAY - 1, k, -1)
                    q = None
                    for source in order:
                        q = q_in[source, rows, :] + (0.0 if q is None else r_in[source, rows, :] * q)
                    behind.append(q)
                q, after_q = behind
                q_all = []
                for i in range(L):
                    own = sec[i, rows, :] * wu[i, rows, :]
                    q = own if q is None else own + pu[i, rows, :] * q
                    q_all.append(q)
                x = q
                if after_q is not None:
                    ep = eu_out[rows, :]
                    p = 1.0 - ep
                    x = (q + p * after_q) / (ep + p * ed_in[rows, :])
                res[L - 1, rows, :] = x
                for i in range(L - 2, -1, -1):
                    x = q_all[i] + pu[i, rows, :] * x
                    res[i, rows, :] = x
                out_copy(c).start()
                return carry

            lax.fori_loop(0, QCH, finish, 0)

    def s_done(o, carry):
        s_copy((col + o) % NCOL, col).wait_send()
        for chunk in range(FCH):
            f_copy(chunk, (col + o) % NCOL, col).wait_send()
        return carry

    lax.fori_loop(1, NCOL, s_done, 0)
    for o in range(1, NGRP):
        g_copy(gcoef, gc_send, gc_recv, (grp + o) % NGRP, grp).wait_send()
        g_copy(gval, gv_send, gv_recv, (grp + o) % NGRP, grp).wait_send()
    for k in range(NLAY):

        @pl.when(lay == k)
        def _():
            for way in range(2):
                for dest in ahead(way, k):
                    if abs(dest - k) == 1:
                        for c in range(ZCH):
                            e_copy(way, c, dest).wait_send()
                    if k in (1, 2):
                        r_copy(way, dest, k).wait_send()
                    for c in range(QCH):
                        q_copy(way, c, dest, k).wait_send()

    for c in range(QCH):
        out_copy(c).wait()


def per_device(salinity, zone_ids, flow_speed, fixed_cells, dispersivity):
    hbm = pl.BlockSpec(memory_space=pl.ANY)
    nat = (L, RB, NCOL * LANES)
    slab = (L, ROWS, LANES)
    by_dest = (NCOL, L, RB, LANES)
    steps = (STEP, LINES, LANES)
    plane = (ROWS, LANES)

    def vm(shape, dtype=F32):
        return pltpu.VMEM(shape, dtype)

    dma = pltpu.SemaphoreType.DMA
    return pl.pallas_call(
        kernel,
        out_shape=jax.ShapeDtypeStruct(slab, F32),
        in_specs=[hbm, hbm, hbm, hbm, pl.BlockSpec(memory_space=pltpu.SMEM)],
        out_specs=hbm,
        scratch_shapes=[
            vm(nat), vm(nat, jnp.int32), vm(nat), vm(nat, jnp.int32),
            vm(by_dest), vm(by_dest), vm(by_dest), vm(slab), vm(slab),
            vm(steps), vm(steps), vm(steps), vm(steps), vm(steps),
            vm(steps), vm(steps), vm(steps), vm(steps), vm(steps),
            vm((5, LINES, LANES)), vm((5, LINES, LANES)), vm((4, LINES, LANES)), vm((4, LINES, LANES)),
            vm((NGRP, 4, L, LANES)), vm((NGRP, 2, L, LANES)),
            vm(slab), vm(slab), vm(slab), vm(slab), vm(slab),
            vm(plane), vm(plane), vm(plane), vm(plane), vm(plane), vm(plane), vm((NLAY,) + plane),
            vm(plane), vm(plane), vm((NLAY,) + plane), vm(slab),
            dma((4,)), dma((NCOL,)), dma((NCOL,)), dma((FCH, NCOL)), dma((FCH, NCOL)),
            dma((NGRP,)), dma((NGRP,)), dma((NGRP,)), dma((NGRP,)),
            dma((2, ZCH)), dma((2, ZCH)), dma((NLAY,)), dma((NLAY,)), dma((QCH, NLAY)), dma((QCH, NLAY)), dma((QCH,)),
        ],
        compiler_params=pltpu.CompilerParams(
            collective_id=0, has_side_effects=True, vmem_limit_bytes=56 * 1024 * 1024
        ),
        name="lod_step",
    )(salinity, zone_ids, flow_speed, fixed_cells, dispersivity)


def solution(mesh):
    placed = P("lay", ("grp", "col"), None)
    return jax.shard_map(
        per_device,
        mesh=mesh,
        in_specs=(placed, placed, placed, placed, P()),
        out_specs=P("lay", "grp", "col"),
        check_vma=False,
    )
```

```python
import jax
import jax.numpy as jnp
from jax import lax
from jax.experimental import pallas as pl
from jax.experimental.pallas import tpu as pltpu
from jax.sharding import PartitionSpec as P

NCOL = 16
NGRP = 4
NLAY = 4
L = 4
RB = 16
LINES = L * RB
LANES = 128
STEP = 16
ROWS = NCOL * RB
ZCH = 4
ZR = ROWS // ZCH
QCH = 4
QR = ROWS // QCH
MESH = pl.DeviceIdType.MESH
F32 = jnp.float32


def butterfly(parts, lane):
    parts = list(parts)
    for m in range(4):
        step = 1 << m
        high = (lane & step) != 0
        for i in range(16):
            if i & step:
                continue
            a, b = parts[i], parts[i + step]
            parts[i] = jnp.where(high, pltpu.roll(b, step, 1), a)
            parts[i + step] = jnp.where(high, b, pltpu.roll(a, LANES - step, 1))
    return parts


def pick(zone, table):
    for m in range(3):
        bit = (zone & (1 << m)) != 0
        table = [jnp.where(bit, table[i + 1], table[i]) for i in range(0, len(table), 2)]
    return table[0]


def kernel(
    sal_hbm, zone_hbm, flow_hbm, fixed_hbm, disp_ref, out_hbm,
    sal, zone, flow, fixed,
    long_nat, st, ft, ct, ys, yf, cy, yb, yc,
    us, uf, up, uq, ur,
    yd, yfd, yp, yw, yr, lev_a, lev_c, lev_i, tmp,
    gcoef, gval,
    sec, wu, pu, wd, pd, eu_in, ed_in, eu_out, ed_out, ru, rd, r_in, qu_out, qd_out, q_in, res,
    in_sem, s_send, s_recv, c_send, c_recv, f_send, f_recv, gc_send, gc_recv, gv_send, gv_recv,
    e_send, e_recv, r_send, r_recv, q_send, q_recv, out_sem,
):
    grp = lax.axis_index("grp")
    col = lax.axis_index("col")
    lay = lax.axis_index("lay")

    def s_copy(dest, source):
        return pltpu.make_async_remote_copy(
            src_ref=st.at[dest],
            dst_ref=ys.at[:, pl.ds(source * RB, RB), :],
            send_sem=s_send.at[dest],
            recv_sem=s_recv.at[source],
            device_id={"col": dest},
            device_id_type=MESH,
        )

    def f_copy(dest, source):
        return pltpu.make_async_remote_copy(
            src_ref=ft.at[dest],
            dst_ref=yf.at[:, pl.ds(source * RB, RB), :],
            send_sem=f_send.at[dest],
            recv_sem=f_recv.at[source],
            device_id={"col": dest},
            device_id_type=MESH,
        )

    def c_copy(dest, source):
        return pltpu.make_async_remote_copy(
            src_ref=ct.at[dest],
            dst_ref=cy.at[source],
            send_sem=c_send.at[dest],
            recv_sem=c_recv.at[source],
            device_id={"col": dest},
            device_id_type=MESH,
        )

    def g_copy(buf, send, recv, dest, source):
        return pltpu.make_async_remote_copy(
            src_ref=buf.at[source],
            dst_ref=buf.at[source],
            send_sem=send.at[dest],
            recv_sem=recv.at[source],
            device_id={"grp": dest},
            device_id_type=MESH,
        )

    def e_copy(way, c, dest):
        rows = pl.ds(pl.multiple_of(c * ZR, ZR), ZR)
        src, dst = ((eu_out, eu_in), (ed_out, ed_in))[way]
        return pltpu.make_async_remote_copy(
            src_ref=src.at[rows],
            dst_ref=dst.at[rows],
            send_sem=e_send.at[way, c],
            recv_sem=e_recv.at[way, c],
            device_id={"lay": dest},
            device_id_type=MESH,
        )

    def r_copy(way, dest):
        return pltpu.make_async_remote_copy(
            src_ref=(ru, rd)[way],
            dst_ref=r_in,
            send_sem=r_send.at[0],
            recv_sem=r_recv.at[0],
            device_id={"lay": dest},
            device_id_type=MESH,
        )

    def q_copy(way, c, dest, source):
        rows = pl.ds(pl.multiple_of(c * QR, QR), QR)
        return pltpu.make_async_remote_copy(
            src_ref=(qu_out, qd_out)[way].at[rows],
            dst_ref=q_in.at[source, rows],
            send_sem=q_send.at[c, dest],
            recv_sem=q_recv.at[c, source],
            device_id={"lay": dest},
            device_id_type=MESH,
        )

    def out_copy(c):
        rows = pl.ds(pl.multiple_of(c * QR, QR), QR)
        return pltpu.make_async_copy(res.at[:, rows, :], out_hbm.at[:, rows, :], out_sem.at[c])

    def ahead(way, k):
        return range(k + 1, NLAY) if way == 0 else range(k - 1, -1, -1)

    whole = (LINES, LANES)

    def to_steps(flat, steps_ref):
        for m in range(LINES // 8):
            for j in range(STEP):
                steps_ref[j, pl.ds(8 * m, 8), :] = flat[pl.ds(8 * STEP * m + j, 8, stride=STEP), :]

    def block_factors(steps_ref, w_ref, p_ref, r_ref):
        e = jnp.ones(whole, F32)
        r = jnp.ones(whole, F32)
        eb = jnp.ones(whole, F32)
        for j in range(1, STEP):
            s = steps_ref[j]
            se = s * e
            w = 1.0 / (1.0 + s + se)
            p = s * w
            e = (1.0 + se) * w
            r_now = r * p
            eb = eb - r * r_now
            r = r_now
            w_ref[j] = w
            p_ref[j] = p
            r_ref[j] = r
        return e, r, eb

    def e_stage(k):
        for way in range(2):

            @pl.when(lay == (k if way == 0 else NLAY - 1 - k))
            def _():
                me = k if way == 0 else NLAY - 1 - k
                src, out, wr, pr, prod = ((eu_in, eu_out, wu, pu, ru), (ed_in, ed_out, wd, pd, rd))[way]

                def step(c, carry):
                    rows = pl.ds(pl.multiple_of(c * ZR, ZR), ZR)
                    if k > 0:
                        e_copy(way, c, me).wait_recv()
                        e = src[rows, :]
                    else:
                        e = jnp.ones((ZR, LANES), F32)
                    total = None
                    for i in range(L) if way == 0 else range(L - 1, -1, -1):
                        s = ys[i, rows, :]
                        se = s * e
                        w = 1.0 / (1.0 + s + se)
                        e = (1.0 + se) * w
                        p = s * w
                        wr[i, rows, :] = w
                        pr[i, rows, :] = p
                        total = p if total is None else total * p
                    out[rows, :] = e
                    prod[rows, :] = total
                    if k < NLAY - 1:
                        e_copy(way, c, ahead(way, me)[0]).start()
                    return carry

                lax.fori_loop(0, ZCH, step, 0)
                if k == 1:
                    r_copy(way, ahead(way, me)[0]).start()

    loads = [
        pltpu.make_async_copy(zone_hbm, zone, in_sem.at[0]),
        pltpu.make_async_copy(flow_hbm, flow, in_sem.at[1]),
        pltpu.make_async_copy(fixed_hbm, fixed, in_sem.at[2]),
        pltpu.make_async_copy(sal_hbm, sal, in_sem.at[3]),
    ]
    for copy in loads:
        copy.start()

    barrier = pltpu.get_barrier_semaphore()

    def greet_col(o, carry):
        pl.semaphore_signal(barrier, inc=1, device_id={"col": (col + o) % NCOL}, device_id_type=MESH)
        return carry

    lax.fori_loop(1, NCOL, greet_col, 0)
    for o in range(1, NGRP):
        pl.semaphore_signal(barrier, inc=1, device_id={"grp": (grp + o) % NGRP}, device_id_type=MESH)
    for o in range(1, NLAY):
        pl.semaphore_signal(barrier, inc=1, device_id={"lay": (lay + o) % NLAY}, device_id_type=MESH)

    lane = lax.broadcasted_iota(jnp.int32, (8, LANES), 1)

    for copy in loads[:3]:
        copy.wait()
    table_long = [disp_ref[0, i] for i in range(8)]
    table_trans = [disp_ref[1, i] for i in range(8)]

    def couple(z, carry):
        for half in range(2):
            rows = pl.ds(8 * half, 8)
            for b in range(NCOL):
                cols = pl.ds(LANES * b, LANES)
                ids = zone[z, rows, cols]
                speed = flow[z, rows, cols]
                opened = 1.0 - fixed[z, rows, cols].astype(F32)
                st[b, z, rows, :] = opened * pick(ids, table_trans) * speed
                long_nat[b, z, rows, :] = opened * pick(ids, table_long) * speed
        return carry

    lax.fori_loop(0, L, couple, 0)

    pl.semaphore_wait(barrier, NCOL - 1 + NGRP - 1 + NLAY - 1)

    def s_start(o, carry):
        s_copy((col + o) % NCOL, col).start()
        return carry

    lax.fori_loop(1, NCOL, s_start, 0)
    ys[:, pl.ds(col * RB, RB), :] = st[col]

    to_steps(st.reshape(NCOL * LINES, LANES), yd)
    block_factors(yd, yw, yp, yr)

    loads[3].wait()

    def spread(z, carry):
        for half in range(2):
            rows = pl.ds(8 * half, 8)
            line = pl.ds(pl.multiple_of(z * RB + 8 * half, 8), 8)
            s_parts = butterfly([long_nat[b, z, rows, :] for b in range(NCOL)], lane)
            for j in range(STEP):
                us[j, line, :] = s_parts[j]
            f_parts = butterfly([sal[z, rows, pl.ds(LANES * b, LANES)] for b in range(NCOL)], lane)
            for j in range(STEP):
                uf[j, line, :] = f_parts[j]
        return carry

    lax.fori_loop(0, L, spread, 0)

    e = jnp.ones(whole, F32)
    r = jnp.ones(whole, F32)
    q = jnp.zeros(whole, F32)
    alpha = jnp.zeros(whole, F32)
    eb = jnp.ones(whole, F32)
    for j in range(1, STEP):
        s = us[j]
        f = uf[j]
        se = s * e
        w = 1.0 / (1.0 + s + se)
        p = s * w
        e = (1.0 + se) * w
        q = f * w + p * q
        r_now = r * p
        alpha = alpha + r * q
        eb = eb - r * r_now
        r = r_now
        up[j] = p
        uq[j] = q
        ur[j] = r

    lanes = lax.broadcasted_iota(jnp.int32, whole, 1)
    sub = lanes // 16
    low = lanes % 16
    first_block = lanes == 0
    last_block = lanes == LANES - 1

    def before(v, d):
        if d >= 8:
            return pltpu.roll(v, d // 8, 1)
        return jnp.where(sub >= d, pltpu.roll(v, 16 * d, 1), pltpu.roll(v, 16 * d + 1, 1))

    def after(v, d):
        if d >= 8:
            return pltpu.roll(v, LANES - d // 8, 1)
        return jnp.where(
            sub < 8 - d, pltpu.roll(v, LANES - 16 * d, 1), pltpu.roll(v, LANES - 16 * d - 1, 1)
        )

    s = us[0]
    ep_left = jnp.where(first_block, 1.0, before(e, 1))
    q_left = jnp.where(first_block, 0.0, before(q, 1))
    r_left = jnp.where(first_block, 0.0, before(r, 1))
    inv = 1.0 / (1.0 + s * (eb + ep_left))
    a = s * r_left * inv
    c = jnp.where(last_block, 0.0, s * r * inv)
    f = (uf[0] + s * (q_left + alpha)) * inv
    for m in range(7):
        d = 1 << m
        inv = 1.0 / (1.0 - a * before(c, d) - c * after(a, d))
        f = (f + a * before(f, d) + c * after(f, d)) * inv
        if m < 6:
            a, c = a * before(a, d) * inv, c * after(c, d) * inv

    uf[0] = f
    x = jnp.where(last_block, 0.0, after(f, 1))
    for j in range(STEP - 1, 0, -1):
        x = uq[j] + ur[j] * f + up[j] * x
        uf[j] = x

    def gather(z, carry):
        for half in range(2):
            rows = pl.ds(8 * half, 8)
            line = pl.ds(pl.multiple_of(z * RB + 8 * half, 8), 8)
            parts = butterfly([uf[j, line, :] for j in range(STEP)], lane)
            for b in range(NCOL):
                ft[b, z, rows, :] = parts[b]
        return carry

    lax.fori_loop(0, L, gather, 0)

    ft_flat = ft.reshape(NCOL * LINES, LANES)
    to_steps(ft_flat, yfd)
    q = yfd[1] * yw[1]
    yfd[1] = q
    alpha = q
    for j in range(2, STEP):
        q = yfd[j] * yw[j] + yp[j] * q
        yfd[j] = q
        alpha = alpha + yr[j - 1] * q
    head = yfd[0] + yd[0] * alpha
    for b in range(NCOL):
        ct[b, 0] = head[L * b : L * (b + 1)]
        ct[b, 1] = q[L * b : L * (b + 1)]

    def c_start(o, carry):
        c_copy((col + o) % NCOL, col).start()
        return carry

    lax.fori_loop(1, NCOL, c_start, 0)
    cy[col] = ct[col]

    x = yfd[STEP - 1]
    for j in range(STEP - 1, -1, -1):
        if j == 0:
            x = jnp.zeros(whole, F32)
        elif j < STEP - 1:
            x = yfd[j] + yp[j] * x
        for m in range(LINES // 8):
            ft_flat[pl.ds(8 * STEP * m + j, 8, stride=STEP), :] = x[8 * m : 8 * m + 8]

    def f_start(o, carry):
        f_copy((col + o) % NCOL, col).start()
        return carry

    lax.fori_loop(1, NCOL, f_start, 0)
    yf[:, pl.ds(col * RB, RB), :] = ft[col]

    def s_wait(o, carry):
        s_copy(col, (col + NCOL - o) % NCOL).wait_recv()
        return carry

    lax.fori_loop(1, NCOL, s_wait, 0)

    e_stage(0)

    to_steps(ys.reshape(L * ROWS, LANES), yd)

    e, r, eb = block_factors(yd, yw, yp, yr)
    block = lax.broadcasted_iota(jnp.int32, whole, 0) % RB

    def above(v, d, edge):
        return jnp.where(block >= d, pltpu.roll(v, d, 0), edge)

    def below(v, d, edge):
        return jnp.where(block < RB - d, pltpu.roll(v, LINES - d, 0), edge)

    s = yd[0]
    inv = 1.0 / (1.0 + s * (eb + above(e, 1, 1.0)))
    a = s * above(r, 1, 1.0) * inv
    c = s * r * inv
    yw[0] = inv
    for m in range(4):
        d = 1 << m
        inv = 1.0 / (1.0 - a * above(c, d, 0.0) - c * below(a, d, 0.0))
        lev_a[m] = a * inv
        lev_c[m] = c * inv
        lev_i[m] = inv
        a, c = a * above(a, d, 1.0) * inv, c * below(c, d, 1.0) * inv
    lev_a[4] = a
    lev_c[4] = c
    top = pl.ds(0, L, stride=RB)
    bottom = pl.ds(RB - 1, L, stride=RB)
    tmp[0] = r * a
    tmp[1] = (1.0 - e) + r * c
    gcoef[grp, 0] = lev_a[4, top, :]
    gcoef[grp, 1] = lev_c[4, top, :]
    gcoef[grp, 2] = tmp[0, bottom, :]
    gcoef[grp, 3] = tmp[1, bottom, :]

    for o in range(1, NGRP):
        g_copy(gcoef, gc_send, gc_recv, (grp + o) % NGRP, grp).start()

    to_left = jnp.zeros(whole, F32)
    to_right = jnp.ones(whole, F32)
    yb_flat = yb.reshape(L * ROWS, LANES)
    yc_flat = yc.reshape(L * ROWS, LANES)
    for j in range(STEP - 1, -1, -1):
        if j == 0:
            to_left, to_right = jnp.ones(whole, F32), jnp.zeros(whole, F32)
        else:
            to_left = yr[j] + yp[j] * to_left
            to_right = yp[j] * to_right
        for m in range(LINES // 8):
            rows = pl.ds(8 * STEP * m + j, 8, stride=STEP)
            yb_flat[rows, :] = to_left[8 * m : 8 * m + 8]
            yc_flat[rows, :] = to_right[8 * m : 8 * m + 8]

    def c_wait(o, carry):
        c_copy(col, (col + NCOL - o) % NCOL).wait_recv()
        return carry

    lax.fori_loop(1, NCOL, c_wait, 0)
    for k in range(NCOL):
        tmp[2, pl.ds(k, L, stride=NCOL), :] = cy[k, 0]
        tmp[3, pl.ds(k, L, stride=NCOL), :] = cy[k, 1]

    q = tmp[3]
    f = (tmp[2] + yd[0] * above(q, 1, 0.0)) * yw[0]
    for m in range(4):
        d = 1 << m
        f = f * lev_i[m] + lev_a[m] * above(f, d, 0.0) + lev_c[m] * below(f, d, 0.0)
    tmp[2] = f
    tmp[3] = q + yr[STEP - 1] * f
    gval[grp, 0] = tmp[2, top, :]
    gval[grp, 1] = tmp[3, bottom, :]

    for o in range(1, NGRP):
        g_copy(gval, gv_send, gv_recv, (grp + o) % NGRP, grp).start()

    e_stage(1)

    for o in range(1, NGRP):
        g_copy(gcoef, gc_send, gc_recv, grp, (grp + NGRP - o) % NGRP).wait_recv()
    for o in range(1, NGRP):
        g_copy(gval, gv_send, gv_recv, grp, (grp + NGRP - o) % NGRP).wait_recv()

    be = [gcoef[g, 0] for g in range(NGRP)]
    ga = [gcoef[g, 1] for g in range(NGRP)]
    rr = [gcoef[g, 2] for g in range(NGRP)]
    pp = [gcoef[g, 3] for g in range(NGRP)]
    al = [gval[g, 0] for g in range(NGRP)]
    qq = [gval[g, 1] for g in range(NGRP)]
    pre_p, pre_q = [pp[0]], [qq[0]]
    for g in range(1, NGRP - 1):
        t = rr[g] / (1.0 - pre_p[-1] * be[g])
        pre_p, pre_q = (
            pre_p + [pp[g] + t * pre_p[-1] * ga[g]],
            pre_q + [qq[g] + t * (pre_q[-1] + pre_p[-1] * al[g])],
        )
    suf_p, suf_q = [be[NGRP - 1]], [al[NGRP - 1]]
    for g in range(NGRP - 2, 0, -1):
        t = ga[g] * suf_p[0] / (1.0 - pp[g] * suf_p[0])
        suf_p, suf_q = (
            [be[g] + t * rr[g]] + suf_p,
            [al[g] + ga[g] * suf_q[0] + t * (qq[g] + pp[g] * suf_q[0])] + suf_q,
        )
    left = jnp.zeros((L, LANES), F32)
    right = jnp.zeros((L, LANES), F32)
    for i in range(NGRP - 1):
        u = (pre_q[i] + pre_p[i] * suf_q[i]) / (1.0 - pre_p[i] * suf_p[i])
        v = suf_q[i] + suf_p[i] * u
        left = jnp.where(grp == i + 1, u, left)
        right = jnp.where(grp == i, v, right)

    def per_line(v):
        return jnp.concatenate([jnp.broadcast_to(v[z : z + 1], (RB, LANES)) for z in range(L)], 0)

    right = per_line(right)
    f = f + lev_a[4] * per_line(left) + lev_c[4] * right
    tmp[2] = f
    tmp[3] = jnp.where(block == RB - 1, right, pltpu.roll(f, LINES - 1, 0))

    def f_wait(o, carry):
        f_copy(col, (col + NCOL - o) % NCOL).wait_recv()
        return carry

    lax.fori_loop(1, NCOL, f_wait, 0)

    def fill(z, carry):
        for k in range(NCOL):
            rows = pl.ds(RB * k, RB)
            here = tmp[2, pl.ds(z * NCOL + k, 1), :]
            there = tmp[3, pl.ds(z * NCOL + k, 1), :]
            sec[z, rows, :] = yf[z, rows, :] + yb[z, rows, :] * here + yc[z, rows, :] * there
        return carry

    lax.fori_loop(0, L, fill, 0)

    for k in range(NLAY):

        @pl.when(lay == k)
        def _():
            way = 0 if k < 2 else 1
            out, wr, pr = ((qu_out, wu, pu), (qd_out, wd, pd))[way]
            order = list(range(L) if way == 0 else range(L - 1, -1, -1))
            dests = [ahead(way, k)[1], ahead(way, k)[0]] if k in (0, NLAY - 1) else [ahead(way, k)[0]]

            def q_local(c, carry):
                rows = pl.ds(pl.multiple_of(c * QR, QR), QR)
                q = sec[order[0], rows, :] * wr[order[0], rows, :]
                for i in order[1:]:
                    q = sec[i, rows, :] * wr[i, rows, :] + pr[i, rows, :] * q
                out[rows, :] = q
                for dest in dests:
                    q_copy(way, c, dest, k).start()
                return carry

            lax.fori_loop(0, QCH, q_local, 0)

    e_stage(2)
    for k in (1, 2):

        @pl.when(lay == k)
        def _():
            way = 0 if k == 2 else 1
            out, wr, pr = ((qu_out, wu, pu), (qd_out, wd, pd))[way]
            order = list(range(L) if way == 0 else range(L - 1, -1, -1))
            near, far = (k - 1, k - 2) if way == 0 else (k + 1, k + 2)
            r_copy(way, k).wait_recv()

            def q_middle(c, carry):
                rows = pl.ds(pl.multiple_of(c * QR, QR), QR)
                q_copy(0, c, k, near).wait_recv()
                q_copy(0, c, k, far).wait_recv()
                q = q_in[near, rows, :] + r_in[rows, :] * q_in[far, rows, :]
                q_in[far, rows, :] = q
                for i in order:
                    q = sec[i, rows, :] * wr[i, rows, :] + pr[i, rows, :] * q
                out[rows, :] = q
                q_copy(way, c, ahead(way, k)[0], k).start()
                return carry

            lax.fori_loop(0, QCH, q_middle, 0)

    e_stage(3)

    for k in range(NLAY):

        @pl.when(lay == k)
        def _():
            below_from = {0: None, 1: 0, 2: 0, 3: 2}[k]
            above_from = {0: 1, 1: 3, 2: 3, 3: None}[k]

            def finish(c, carry):
                rows = pl.ds(pl.multiple_of(c * QR, QR), QR)
                own = {0: 1, 1: 0, 2: 3, 3: 2}[k]
                q_copy(0, c, k, own).wait_recv()
                q = None if below_from is None else q_in[below_from, rows, :]
                q_all = []
                for i in range(L):
                    mine = sec[i, rows, :] * wu[i, rows, :]
                    q = mine if q is None else mine + pu[i, rows, :] * q
                    q_all.append(q)
                x = q
                if above_from is not None:
                    ep = eu_out[rows, :]
                    p = 1.0 - ep
                    x = (q + p * q_in[above_from, rows, :]) / (ep + p * ed_in[rows, :])
                res[L - 1, rows, :] = x
                for i in range(L - 2, -1, -1):
                    x = q_all[i] + pu[i, rows, :] * x
                    res[i, rows, :] = x
                out_copy(c).start()
                return carry

            lax.fori_loop(0, QCH, finish, 0)

    def s_done(o, carry):
        s_copy((col + o) % NCOL, col).wait_send()
        c_copy((col + o) % NCOL, col).wait_send()
        f_copy((col + o) % NCOL, col).wait_send()
        return carry

    lax.fori_loop(1, NCOL, s_done, 0)
    for o in range(1, NGRP):
        g_copy(gcoef, gc_send, gc_recv, (grp + o) % NGRP, grp).wait_send()
        g_copy(gval, gv_send, gv_recv, (grp + o) % NGRP, grp).wait_send()
    for k in range(NLAY):

        @pl.when(lay == k)
        def _():
            for way in range(2):
                back = k if way == 0 else NLAY - 1 - k
                if back == NLAY - 1:
                    continue
                dest = ahead(way, k)[0]
                for c in range(ZCH):
                    e_copy(way, c, dest).wait_send()
                if back == 1:
                    r_copy(way, dest).wait_send()
                for c in range(QCH):
                    q_copy(way, c, dest, k).wait_send()
                    if back == 0:
                        q_copy(way, c, ahead(way, k)[1], k).wait_send()

    for c in range(QCH):
        out_copy(c).wait()


def per_device(salinity, zone_ids, flow_speed, fixed_cells, dispersivity):
    hbm = pl.BlockSpec(memory_space=pl.ANY)
    nat = (L, RB, NCOL * LANES)
    slab = (L, ROWS, LANES)
    by_dest = (NCOL, L, RB, LANES)
    steps = (STEP, LINES, LANES)
    plane = (ROWS, LANES)

    def vm(shape, dtype=F32):
        return pltpu.VMEM(shape, dtype)

    dma = pltpu.SemaphoreType.DMA
    return pl.pallas_call(
        kernel,
        out_shape=jax.ShapeDtypeStruct(slab, F32),
        in_specs=[hbm, hbm, hbm, hbm, pl.BlockSpec(memory_space=pltpu.SMEM)],
        out_specs=hbm,
        scratch_shapes=[
            vm(nat), vm(nat, jnp.int32), vm(nat), vm(nat, jnp.int32),
            vm(by_dest), vm(by_dest), vm(by_dest), vm((NCOL, 2, L, LANES)), vm(slab), vm(slab),
            vm((NCOL, 2, L, LANES)), vm(slab), vm(slab),
            vm(steps), vm(steps), vm(steps), vm(steps), vm(steps),
            vm(steps), vm(steps), vm(steps), vm(steps), vm(steps),
            vm((5, LINES, LANES)), vm((5, LINES, LANES)), vm((4, LINES, LANES)), vm((4, LINES, LANES)),
            vm((NGRP, 4, L, LANES)), vm((NGRP, 2, L, LANES)),
            vm(slab), vm(slab), vm(slab), vm(slab), vm(slab),
            vm(plane), vm(plane), vm(plane), vm(plane), vm(plane), vm(plane), vm(plane),
            vm(plane), vm(plane), vm((NLAY,) + plane), vm(slab),
            dma((4,)), dma((NCOL,)), dma((NCOL,)), dma((NCOL,)), dma((NCOL,)), dma((NCOL,)), dma((NCOL,)),
            dma((NGRP,)), dma((NGRP,)), dma((NGRP,)), dma((NGRP,)),
            dma((2, ZCH)), dma((2, ZCH)), dma((1,)), dma((1,)), dma((QCH, NLAY)), dma((QCH, NLAY)), dma((QCH,)),
        ],
        compiler_params=pltpu.CompilerParams(
            collective_id=0, has_side_effects=True, vmem_limit_bytes=56 * 1024 * 1024
        ),
        name="lod_step",
    )(salinity, zone_ids, flow_speed, fixed_cells, dispersivity)


def solution(mesh):
    placed = P("lay", ("grp", "col"), None)
    return jax.shard_map(
        per_device,
        mesh=mesh,
        in_specs=(placed, placed, placed, placed, P()),
        out_specs=P("lay", "grp", "col"),
        check_vma=False,
    )
```

```python
import jax
import jax.numpy as jnp
from jax import lax
from jax.experimental import pallas as pl
from jax.experimental.pallas import tpu as pltpu
from jax.sharding import PartitionSpec as P

NCOL = 16
NGRP = 4
NLAY = 4
L = 4
RB = 16
LINES = L * RB
LANES = 128
STEP = 16
ROWS = NCOL * RB
ZCH = 4
ZR = ROWS // ZCH
QCH = 4
QR = ROWS // QCH
MESH = pl.DeviceIdType.MESH
F32 = jnp.float32


def butterfly(parts, lane):
    parts = list(parts)
    for m in range(4):
        step = 1 << m
        high = (lane & step) != 0
        for i in range(16):
            if i & step:
                continue
            a, b = parts[i], parts[i + step]
            parts[i] = jnp.where(high, pltpu.roll(b, step, 1), a)
            parts[i + step] = jnp.where(high, b, pltpu.roll(a, LANES - step, 1))
    return parts


def pick(zone, table):
    for m in range(3):
        bit = (zone & (1 << m)) != 0
        table = [jnp.where(bit, table[i + 1], table[i]) for i in range(0, len(table), 2)]
    return table[0]


def kernel(
    sal_hbm, zone_hbm, flow_hbm, fixed_hbm, disp_ref, out_hbm,
    sal, zone, flow, fixed,
    long_nat, st, ft, ct, ys, yf, cy, yb, yc,
    us, uf, up, uq, ur,
    yd, yfd, yp, yw, yr, lev_a, lev_c, lev_i, tmp,
    gcoef, gval,
    sec, wu, pu, wd, pd, eu_in, ed_in, eu_out, ed_out, ru, rd, r_in, qu_out, qd_out, q_in, res,
    in_sem, s_send, s_recv, c_send, c_recv, f_send, f_recv, gc_send, gc_recv, gv_send, gv_recv,
    e_send, e_recv, r_send, r_recv, q_send, q_recv, out_sem,
):
    grp = lax.axis_index("grp")
    col = lax.axis_index("col")
    lay = lax.axis_index("lay")

    def s_copy(dest, source):
        return pltpu.make_async_remote_copy(
            src_ref=st.at[dest],
            dst_ref=ys.at[:, pl.ds(source * RB, RB), :],
            send_sem=s_send.at[dest],
            recv_sem=s_recv.at[source],
            device_id={"col": dest},
            device_id_type=MESH,
        )

    def f_copy(dest, source):
        return pltpu.make_async_remote_copy(
            src_ref=ft.at[dest],
            dst_ref=yf.at[:, pl.ds(source * RB, RB), :],
            send_sem=f_send.at[dest],
            recv_sem=f_recv.at[source],
            device_id={"col": dest},
            device_id_type=MESH,
        )

    def c_copy(dest, source):
        return pltpu.make_async_remote_copy(
            src_ref=ct.at[dest],
            dst_ref=cy.at[source],
            send_sem=c_send.at[dest],
            recv_sem=c_recv.at[source],
            device_id={"col": dest},
            device_id_type=MESH,
        )

    def g_copy(buf, send, recv, dest, source):
        return pltpu.make_async_remote_copy(
            src_ref=buf.at[source],
            dst_ref=buf.at[source],
            send_sem=send.at[dest],
            recv_sem=recv.at[source],
            device_id={"grp": dest},
            device_id_type=MESH,
        )

    def e_copy(way, c, dest):
        rows = pl.ds(pl.multiple_of(c * ZR, ZR), ZR)
        src, dst = ((eu_out, eu_in), (ed_out, ed_in))[way]
        return pltpu.make_async_remote_copy(
            src_ref=src.at[rows],
            dst_ref=dst.at[rows],
            send_sem=e_send.at[way, c],
            recv_sem=e_recv.at[way, c],
            device_id={"lay": dest},
            device_id_type=MESH,
        )

    def r_copy(way, dest):
        return pltpu.make_async_remote_copy(
            src_ref=(ru, rd)[way],
            dst_ref=r_in,
            send_sem=r_send.at[0],
            recv_sem=r_recv.at[0],
            device_id={"lay": dest},
            device_id_type=MESH,
        )

    def q_copy(way, c, dest, source):
        rows = pl.ds(pl.multiple_of(c * QR, QR), QR)
        return pltpu.make_async_remote_copy(
            src_ref=(qu_out, qd_out)[way].at[rows],
            dst_ref=q_in.at[source, rows],
            send_sem=q_send.at[c, dest],
            recv_sem=q_recv.at[c, source],
            device_id={"lay": dest},
            device_id_type=MESH,
        )

    def out_copy(c):
        rows = pl.ds(pl.multiple_of(c * QR, QR), QR)
        return pltpu.make_async_copy(res.at[:, rows, :], out_hbm.at[:, rows, :], out_sem.at[c])

    def ahead(way, k):
        return range(k + 1, NLAY) if way == 0 else range(k - 1, -1, -1)

    whole = (LINES, LANES)

    def to_steps(flat, steps_ref):
        for m in range(LINES // 8):
            for j in range(STEP):
                steps_ref[j, pl.ds(8 * m, 8), :] = flat[pl.ds(8 * STEP * m + j, 8, stride=STEP), :]

    def block_factors(steps_ref, w_ref, p_ref, r_ref):
        e = jnp.ones(whole, F32)
        r = jnp.ones(whole, F32)
        eb = jnp.ones(whole, F32)
        for j in range(1, STEP):
            s = steps_ref[j]
            se = s * e
            w = 1.0 / (1.0 + s + se)
            p = s * w
            e = (1.0 + se) * w
            r_now = r * p
            eb = eb - r * r_now
            r = r_now
            w_ref[j] = w
            p_ref[j] = p
            r_ref[j] = r
        return e, r, eb

    def e_stage(k):
        for way in range(2):

            @pl.when(lay == (k if way == 0 else NLAY - 1 - k))
            def _():
                me = k if way == 0 else NLAY - 1 - k
                src, out, wr, pr, prod = ((eu_in, eu_out, wu, pu, ru), (ed_in, ed_out, wd, pd, rd))[way]

                def step(c, carry):
                    rows = pl.ds(pl.multiple_of(c * ZR, ZR), ZR)
                    if k > 0:
                        e_copy(way, c, me).wait_recv()
                        e = src[rows, :]
                    else:
                        e = jnp.ones((ZR, LANES), F32)
                    total = None
                    for i in range(L) if way == 0 else range(L - 1, -1, -1):
                        s = ys[i, rows, :]
                        se = s * e
                        w = 1.0 / (1.0 + s + se)
                        e = (1.0 + se) * w
                        p = s * w
                        wr[i, rows, :] = w
                        pr[i, rows, :] = p
                        total = p if total is None else total * p
                    out[rows, :] = e
                    prod[rows, :] = total
                    if k < NLAY - 1:
                        e_copy(way, c, ahead(way, me)[0]).start()
                    return carry

                lax.fori_loop(0, ZCH, step, 0)

    loads = [
        pltpu.make_async_copy(zone_hbm, zone, in_sem.at[0]),
        pltpu.make_async_copy(flow_hbm, flow, in_sem.at[1]),
        pltpu.make_async_copy(fixed_hbm, fixed, in_sem.at[2]),
        pltpu.make_async_copy(sal_hbm, sal, in_sem.at[3]),
    ]
    for copy in loads:
        copy.start()

    barrier = pltpu.get_barrier_semaphore()

    def greet_col(o, carry):
        pl.semaphore_signal(barrier, inc=1, device_id={"col": (col + o) % NCOL}, device_id_type=MESH)
        return carry

    lax.fori_loop(1, NCOL, greet_col, 0)
    for o in range(1, NGRP):
        pl.semaphore_signal(barrier, inc=1, device_id={"grp": (grp + o) % NGRP}, device_id_type=MESH)
    for o in range(1, NLAY):
        pl.semaphore_signal(barrier, inc=1, device_id={"lay": (lay + o) % NLAY}, device_id_type=MESH)

    lane = lax.broadcasted_iota(jnp.int32, (8, LANES), 1)

    for copy in loads[:3]:
        copy.wait()
    table_long = [disp_ref[0, i] for i in range(8)]
    table_trans = [disp_ref[1, i] for i in range(8)]

    def couple(z, carry):
        for half in range(2):
            rows = pl.ds(8 * half, 8)
            for b in range(NCOL):
                cols = pl.ds(LANES * b, LANES)
                ids = zone[z, rows, cols]
                speed = flow[z, rows, cols]
                opened = 1.0 - fixed[z, rows, cols].astype(F32)
                st[b, z, rows, :] = opened * pick(ids, table_trans) * speed
                long_nat[b, z, rows, :] = opened * pick(ids, table_long) * speed
        return carry

    lax.fori_loop(0, L, couple, 0)

    pl.semaphore_wait(barrier, NCOL - 1 + NGRP - 1 + NLAY - 1)

    def s_start(o, carry):
        s_copy((col + o) % NCOL, col).start()
        return carry

    lax.fori_loop(1, NCOL, s_start, 0)
    ys[:, pl.ds(col * RB, RB), :] = st[col]

    to_steps(st.reshape(NCOL * LINES, LANES), yd)
    block_factors(yd, yw, yp, yr)

    loads[3].wait()

    def spread(z, carry):
        for half in range(2):
            rows = pl.ds(8 * half, 8)
            line = pl.ds(pl.multiple_of(z * RB + 8 * half, 8), 8)
            s_parts = butterfly([long_nat[b, z, rows, :] for b in range(NCOL)], lane)
            for j in range(STEP):
                us[j, line, :] = s_parts[j]
            f_parts = butterfly([sal[z, rows, pl.ds(LANES * b, LANES)] for b in range(NCOL)], lane)
            for j in range(STEP):
                uf[j, line, :] = f_parts[j]
        return carry

    lax.fori_loop(0, L, spread, 0)

    e = jnp.ones(whole, F32)
    r = jnp.ones(whole, F32)
    q = jnp.zeros(whole, F32)
    alpha = jnp.zeros(whole, F32)
    eb = jnp.ones(whole, F32)
    for j in range(1, STEP):
        s = us[j]
        f = uf[j]
        se = s * e
        w = 1.0 / (1.0 + s + se)
        p = s * w
        e = (1.0 + se) * w
        q = f * w + p * q
        r_now = r * p
        alpha = alpha + r * q
        eb = eb - r * r_now
        r = r_now
        up[j] = p
        uq[j] = q
        ur[j] = r

    lanes = lax.broadcasted_iota(jnp.int32, whole, 1)
    sub = lanes // 16
    low = lanes % 16
    first_block = lanes == 0
    last_block = lanes == LANES - 1

    def before(v, d):
        if d >= 8:
            return pltpu.roll(v, d // 8, 1)
        return jnp.where(sub >= d, pltpu.roll(v, 16 * d, 1), pltpu.roll(v, 16 * d + 1, 1))

    def after(v, d):
        if d >= 8:
            return pltpu.roll(v, LANES - d // 8, 1)
        return jnp.where(
            sub < 8 - d, pltpu.roll(v, LANES - 16 * d, 1), pltpu.roll(v, LANES - 16 * d - 1, 1)
        )

    s = us[0]
    ep_left = jnp.where(first_block, 1.0, before(e, 1))
    q_left = jnp.where(first_block, 0.0, before(q, 1))
    r_left = jnp.where(first_block, 0.0, before(r, 1))
    inv = 1.0 / (1.0 + s * (eb + ep_left))
    a = s * r_left * inv
    c = jnp.where(last_block, 0.0, s * r * inv)
    f = (uf[0] + s * (q_left + alpha)) * inv
    for m in range(7):
        d = 1 << m
        inv = 1.0 / (1.0 - a * before(c, d) - c * after(a, d))
        f = (f + a * before(f, d) + c * after(f, d)) * inv
        if m < 6:
            a, c = a * before(a, d) * inv, c * after(c, d) * inv

    uf[0] = f
    x = jnp.where(last_block, 0.0, after(f, 1))
    for j in range(STEP - 1, 0, -1):
        x = uq[j] + ur[j] * f + up[j] * x
        uf[j] = x

    def gather(z, carry):
        for half in range(2):
            rows = pl.ds(8 * half, 8)
            line = pl.ds(pl.multiple_of(z * RB + 8 * half, 8), 8)
            parts = butterfly([uf[j, line, :] for j in range(STEP)], lane)
            for b in range(NCOL):
                ft[b, z, rows, :] = parts[b]
        return carry

    lax.fori_loop(0, L, gather, 0)

    ft_flat = ft.reshape(NCOL * LINES, LANES)
    to_steps(ft_flat, yfd)
    q = yfd[1] * yw[1]
    yfd[1] = q
    alpha = q
    for j in range(2, STEP):
        q = yfd[j] * yw[j] + yp[j] * q
        yfd[j] = q
        alpha = alpha + yr[j - 1] * q
    head = yfd[0] + yd[0] * alpha
    for b in range(NCOL):
        ct[b, 0] = head[L * b : L * (b + 1)]
        ct[b, 1] = q[L * b : L * (b + 1)]

    def c_start(o, carry):
        c_copy((col + o) % NCOL, col).start()
        return carry

    lax.fori_loop(1, NCOL, c_start, 0)
    cy[col] = ct[col]

    x = yfd[STEP - 1]
    for j in range(STEP - 1, -1, -1):
        if j == 0:
            x = jnp.zeros(whole, F32)
        elif j < STEP - 1:
            x = yfd[j] + yp[j] * x
        for m in range(LINES // 8):
            ft_flat[pl.ds(8 * STEP * m + j, 8, stride=STEP), :] = x[8 * m : 8 * m + 8]

    def f_start(o, carry):
        f_copy((col + o) % NCOL, col).start()
        return carry

    lax.fori_loop(1, NCOL, f_start, 0)
    yf[:, pl.ds(col * RB, RB), :] = ft[col]

    def s_wait(o, carry):
        s_copy(col, (col + NCOL - o) % NCOL).wait_recv()
        return carry

    lax.fori_loop(1, NCOL, s_wait, 0)

    e_stage(0)

    to_steps(ys.reshape(L * ROWS, LANES), yd)

    e, r, eb = block_factors(yd, yw, yp, yr)
    block = lax.broadcasted_iota(jnp.int32, whole, 0) % RB

    def above(v, d, edge):
        return jnp.where(block >= d, pltpu.roll(v, d, 0), edge)

    def below(v, d, edge):
        return jnp.where(block < RB - d, pltpu.roll(v, LINES - d, 0), edge)

    s = yd[0]
    inv = 1.0 / (1.0 + s * (eb + above(e, 1, 1.0)))
    a = s * above(r, 1, 1.0) * inv
    c = s * r * inv
    yw[0] = inv
    for m in range(4):
        d = 1 << m
        inv = 1.0 / (1.0 - a * above(c, d, 0.0) - c * below(a, d, 0.0))
        lev_a[m] = a * inv
        lev_c[m] = c * inv
        lev_i[m] = inv
        a, c = a * above(a, d, 1.0) * inv, c * below(c, d, 1.0) * inv
    lev_a[4] = a
    lev_c[4] = c
    top = pl.ds(0, L, stride=RB)
    bottom = pl.ds(RB - 1, L, stride=RB)
    tmp[0] = r * a
    tmp[1] = (1.0 - e) + r * c
    gcoef[grp, 0] = lev_a[4, top, :]
    gcoef[grp, 1] = lev_c[4, top, :]
    gcoef[grp, 2] = tmp[0, bottom, :]
    gcoef[grp, 3] = tmp[1, bottom, :]

    for o in range(1, NGRP):
        g_copy(gcoef, gc_send, gc_recv, (grp + o) % NGRP, grp).start()

    to_left = jnp.zeros(whole, F32)
    to_right = jnp.ones(whole, F32)
    yb_flat = yb.reshape(L * ROWS, LANES)
    yc_flat = yc.reshape(L * ROWS, LANES)
    for j in range(STEP - 1, -1, -1):
        if j == 0:
            to_left, to_right = jnp.ones(whole, F32), jnp.zeros(whole, F32)
        else:
            to_left = yr[j] + yp[j] * to_left
            to_right = yp[j] * to_right
        for m in range(LINES // 8):
            rows = pl.ds(8 * STEP * m + j, 8, stride=STEP)
            yb_flat[rows, :] = to_left[8 * m : 8 * m + 8]
            yc_flat[rows, :] = to_right[8 * m : 8 * m + 8]

    def c_wait(o, carry):
        c_copy(col, (col + NCOL - o) % NCOL).wait_recv()
        return carry

    lax.fori_loop(1, NCOL, c_wait, 0)
    for k in range(NCOL):
        tmp[2, pl.ds(k, L, stride=NCOL), :] = cy[k, 0]
        tmp[3, pl.ds(k, L, stride=NCOL), :] = cy[k, 1]

    q = tmp[3]
    f = (tmp[2] + yd[0] * above(q, 1, 0.0)) * yw[0]
    for m in range(4):
        d = 1 << m
        f = f * lev_i[m] + lev_a[m] * above(f, d, 0.0) + lev_c[m] * below(f, d, 0.0)
    tmp[2] = f
    tmp[3] = q + yr[STEP - 1] * f
    gval[grp, 0] = tmp[2, top, :]
    gval[grp, 1] = tmp[3, bottom, :]

    for o in range(1, NGRP):
        g_copy(gval, gv_send, gv_recv, (grp + o) % NGRP, grp).start()

    e_stage(1)

    for o in range(1, NGRP):
        g_copy(gcoef, gc_send, gc_recv, grp, (grp + NGRP - o) % NGRP).wait_recv()
    for o in range(1, NGRP):
        g_copy(gval, gv_send, gv_recv, grp, (grp + NGRP - o) % NGRP).wait_recv()

    be = [gcoef[g, 0] for g in range(NGRP)]
    ga = [gcoef[g, 1] for g in range(NGRP)]
    rr = [gcoef[g, 2] for g in range(NGRP)]
    pp = [gcoef[g, 3] for g in range(NGRP)]
    al = [gval[g, 0] for g in range(NGRP)]
    qq = [gval[g, 1] for g in range(NGRP)]
    pre_p, pre_q = [pp[0]], [qq[0]]
    for g in range(1, NGRP - 1):
        t = rr[g] / (1.0 - pre_p[-1] * be[g])
        pre_p, pre_q = (
            pre_p + [pp[g] + t * pre_p[-1] * ga[g]],
            pre_q + [qq[g] + t * (pre_q[-1] + pre_p[-1] * al[g])],
        )
    suf_p, suf_q = [be[NGRP - 1]], [al[NGRP - 1]]
    for g in range(NGRP - 2, 0, -1):
        t = ga[g] * suf_p[0] / (1.0 - pp[g] * suf_p[0])
        suf_p, suf_q = (
            [be[g] + t * rr[g]] + suf_p,
            [al[g] + ga[g] * suf_q[0] + t * (qq[g] + pp[g] * suf_q[0])] + suf_q,
        )
    left = jnp.zeros((L, LANES), F32)
    right = jnp.zeros((L, LANES), F32)
    for i in range(NGRP - 1):
        u = (pre_q[i] + pre_p[i] * suf_q[i]) / (1.0 - pre_p[i] * suf_p[i])
        v = suf_q[i] + suf_p[i] * u
        left = jnp.where(grp == i + 1, u, left)
        right = jnp.where(grp == i, v, right)

    def per_line(v):
        return jnp.concatenate([jnp.broadcast_to(v[z : z + 1], (RB, LANES)) for z in range(L)], 0)

    right = per_line(right)
    f = f + lev_a[4] * per_line(left) + lev_c[4] * right
    tmp[2] = f
    tmp[3] = jnp.where(block == RB - 1, right, pltpu.roll(f, LINES - 1, 0))

    def f_wait(o, carry):
        f_copy(col, (col + NCOL - o) % NCOL).wait_recv()
        return carry

    lax.fori_loop(1, NCOL, f_wait, 0)

    def fill(z, carry):
        for k in range(NCOL):
            rows = pl.ds(RB * k, RB)
            here = tmp[2, pl.ds(z * NCOL + k, 1), :]
            there = tmp[3, pl.ds(z * NCOL + k, 1), :]
            sec[z, rows, :] = yf[z, rows, :] + yb[z, rows, :] * here + yc[z, rows, :] * there
        return carry

    lax.fori_loop(0, L, fill, 0)

    def q_pass(k, way, back):
        out, wr, pr = ((qu_out, wu, pu), (qd_out, wd, pd))[way]
        order = list(range(L) if way == 0 else range(L - 1, -1, -1))
        behind = k - 1 if way == 0 else k + 1

        def step(c, carry):
            rows = pl.ds(pl.multiple_of(c * QR, QR), QR)
            if back > 0:
                q_copy(0, c, k, behind).wait_recv()
                q = q_in[behind, rows, :]
            for i in order:
                mine = sec[i, rows, :] * wr[i, rows, :]
                q = mine if (back == 0 and i == order[0]) else mine + pr[i, rows, :] * q
            out[rows, :] = q
            q_copy(way, c, ahead(way, k)[0], k).start()
            return carry

        lax.fori_loop(0, QCH, step, 0)

    for k, way, back in ((0, 0, 0), (1, 0, 1), (2, 1, 1), (3, 1, 0)):

        @pl.when(lay == k)
        def _():
            q_pass(k, way, back)

    e_stage(2)
    for k, way in ((1, 1), (2, 0)):

        @pl.when(lay == k)
        def _():
            q_pass(k, way, 2)

    e_stage(3)

    for k in range(NLAY):

        @pl.when(lay == k)
        def _():
            below_from = {0: None, 1: 0, 2: 1, 3: 2}[k]
            above_from = {0: 1, 1: 2, 2: 3, 3: None}[k]

            def finish(c, carry):
                rows = pl.ds(pl.multiple_of(c * QR, QR), QR)
                if k in (0, NLAY - 1):
                    q_copy(0, c, k, 1 if k == 0 else 2).wait_recv()
                q = None if below_from is None else q_in[below_from, rows, :]
                q_all = []
                for i in range(L):
                    mine = sec[i, rows, :] * wu[i, rows, :]
                    q = mine if q is None else mine + pu[i, rows, :] * q
                    q_all.append(q)
                x = q
                if above_from is not None:
                    ep = eu_out[rows, :]
                    p = 1.0 - ep
                    x = (q + p * q_in[above_from, rows, :]) / (ep + p * ed_in[rows, :])
                res[L - 1, rows, :] = x
                for i in range(L - 2, -1, -1):
                    x = q_all[i] + pu[i, rows, :] * x
                    res[i, rows, :] = x
                out_copy(c).start()
                return carry

            lax.fori_loop(0, QCH, finish, 0)

    def s_done(o, carry):
        s_copy((col + o) % NCOL, col).wait_send()
        c_copy((col + o) % NCOL, col).wait_send()
        f_copy((col + o) % NCOL, col).wait_send()
        return carry

    lax.fori_loop(1, NCOL, s_done, 0)
    for o in range(1, NGRP):
        g_copy(gcoef, gc_send, gc_recv, (grp + o) % NGRP, grp).wait_send()
        g_copy(gval, gv_send, gv_recv, (grp + o) % NGRP, grp).wait_send()
    for k in range(NLAY):

        @pl.when(lay == k)
        def _():
            for way in range(2):
                back = k if way == 0 else NLAY - 1 - k
                if back == NLAY - 1:
                    continue
                dest = ahead(way, k)[0]
                for c in range(ZCH):
                    e_copy(way, c, dest).wait_send()
                for c in range(QCH):
                    q_copy(way, c, dest, k).wait_send()

    for c in range(QCH):
        out_copy(c).wait()


def per_device(salinity, zone_ids, flow_speed, fixed_cells, dispersivity):
    hbm = pl.BlockSpec(memory_space=pl.ANY)
    nat = (L, RB, NCOL * LANES)
    slab = (L, ROWS, LANES)
    by_dest = (NCOL, L, RB, LANES)
    steps = (STEP, LINES, LANES)
    plane = (ROWS, LANES)

    def vm(shape, dtype=F32):
        return pltpu.VMEM(shape, dtype)

    dma = pltpu.SemaphoreType.DMA
    return pl.pallas_call(
        kernel,
        out_shape=jax.ShapeDtypeStruct(slab, F32),
        in_specs=[hbm, hbm, hbm, hbm, pl.BlockSpec(memory_space=pltpu.SMEM)],
        out_specs=hbm,
        scratch_shapes=[
            vm(nat), vm(nat, jnp.int32), vm(nat), vm(nat, jnp.int32),
            vm(by_dest), vm(by_dest), vm(by_dest), vm((NCOL, 2, L, LANES)), vm(slab), vm(slab),
            vm((NCOL, 2, L, LANES)), vm(slab), vm(slab),
            vm(steps), vm(steps), vm(steps), vm(steps), vm(steps),
            vm(steps), vm(steps), vm(steps), vm(steps), vm(steps),
            vm((5, LINES, LANES)), vm((5, LINES, LANES)), vm((4, LINES, LANES)), vm((4, LINES, LANES)),
            vm((NGRP, 4, L, LANES)), vm((NGRP, 2, L, LANES)),
            vm(slab), vm(slab), vm(slab), vm(slab), vm(slab),
            vm(plane), vm(plane), vm(plane), vm(plane), vm(plane), vm(plane), vm(plane),
            vm(plane), vm(plane), vm((NLAY,) + plane), vm(slab),
            dma((4,)), dma((NCOL,)), dma((NCOL,)), dma((NCOL,)), dma((NCOL,)), dma((NCOL,)), dma((NCOL,)),
            dma((NGRP,)), dma((NGRP,)), dma((NGRP,)), dma((NGRP,)),
            dma((2, ZCH)), dma((2, ZCH)), dma((1,)), dma((1,)), dma((QCH, NLAY)), dma((QCH, NLAY)), dma((QCH,)),
        ],
        compiler_params=pltpu.CompilerParams(
            collective_id=0, has_side_effects=True, vmem_limit_bytes=56 * 1024 * 1024
        ),
        name="lod_step",
    )(salinity, zone_ids, flow_speed, fixed_cells, dispersivity)


def solution(mesh):
    placed = P("lay", ("grp", "col"), None)
    return jax.shard_map(
        per_device,
        mesh=mesh,
        in_specs=(placed, placed, placed, placed, P()),
        out_specs=P("lay", "grp", "col"),
        check_vma=False,
    )
```

```python
import jax
import jax.numpy as jnp
from jax import lax
from jax.experimental import pallas as pl
from jax.experimental.pallas import tpu as pltpu
from jax.sharding import PartitionSpec as P

NCOL = 16
NGRP = 4
NLAY = 4
L = 4
RB = 16
LINES = L * RB
LANES = 128
STEP = 16
ROWS = NCOL * RB
ZCH = 4
ZR = ROWS // ZCH
QCH = 4
QR = ROWS // QCH
MESH = pl.DeviceIdType.MESH
F32 = jnp.float32


def butterfly(parts, lane):
    parts = list(parts)
    for m in range(4):
        step = 1 << m
        high = (lane & step) != 0
        for i in range(16):
            if i & step:
                continue
            a, b = parts[i], parts[i + step]
            parts[i] = jnp.where(high, pltpu.roll(b, step, 1), a)
            parts[i + step] = jnp.where(high, b, pltpu.roll(a, LANES - step, 1))
    return parts


def pick(zone, table):
    for m in range(3):
        bit = (zone & (1 << m)) != 0
        table = [jnp.where(bit, table[i + 1], table[i]) for i in range(0, len(table), 2)]
    return table[0]


def kernel(
    sal_hbm, zone_hbm, flow_hbm, fixed_hbm, disp_ref, out_hbm,
    sal, zone, flow, fixed,
    long_nat, st, ft, ct, ys, yf, cy, yb, yc,
    us, uf, up, uq, ur,
    yd, yfd, yp, yw, yr, lev_a, lev_c, lev_i, tmp,
    gcoef, gval,
    sec, wu, pu, wd, pd, eu_in, ed_in, eu_out, ed_out, ru, rd, r_in, qu_out, qd_out, q_in, res,
    in_sem, s_send, s_recv, c_send, c_recv, f_send, f_recv, gc_send, gc_recv, gv_send, gv_recv,
    e_send, e_recv, r_send, r_recv, q_send, q_recv, out_sem,
):
    grp = lax.axis_index("grp")
    col = lax.axis_index("col")
    lay = lax.axis_index("lay")

    def s_copy(dest, source):
        return pltpu.make_async_remote_copy(
            src_ref=st.at[dest],
            dst_ref=ys.at[:, pl.ds(source * RB, RB), :],
            send_sem=s_send.at[dest],
            recv_sem=s_recv.at[source],
            device_id={"col": dest},
            device_id_type=MESH,
        )

    def f_copy(dest, source):
        return pltpu.make_async_remote_copy(
            src_ref=ft.at[dest],
            dst_ref=yf.at[:, pl.ds(source * RB, RB), :],
            send_sem=f_send.at[dest],
            recv_sem=f_recv.at[source],
            device_id={"col": dest},
            device_id_type=MESH,
        )

    def c_copy(dest, source):
        return pltpu.make_async_remote_copy(
            src_ref=ct.at[dest],
            dst_ref=cy.at[source],
            send_sem=c_send.at[dest],
            recv_sem=c_recv.at[source],
            device_id={"col": dest},
            device_id_type=MESH,
        )

    def g_copy(buf, send, recv, dest, source):
        return pltpu.make_async_remote_copy(
            src_ref=buf.at[source],
            dst_ref=buf.at[source],
            send_sem=send.at[dest],
            recv_sem=recv.at[source],
            device_id={"grp": dest},
            device_id_type=MESH,
        )

    def e_copy(way, c, dest):
        rows = pl.ds(pl.multiple_of(c * ZR, ZR), ZR)
        src, dst = ((eu_out, eu_in), (ed_out, ed_in))[way]
        return pltpu.make_async_remote_copy(
            src_ref=src.at[rows],
            dst_ref=dst.at[rows],
            send_sem=e_send.at[way, c],
            recv_sem=e_recv.at[way, c],
            device_id={"lay": dest},
            device_id_type=MESH,
        )

    def r_copy(way, dest):
        return pltpu.make_async_remote_copy(
            src_ref=(ru, rd)[way],
            dst_ref=r_in,
            send_sem=r_send.at[0],
            recv_sem=r_recv.at[0],
            device_id={"lay": dest},
            device_id_type=MESH,
        )

    def q_copy(way, c, dest, source):
        rows = pl.ds(pl.multiple_of(c * QR, QR), QR)
        return pltpu.make_async_remote_copy(
            src_ref=(qu_out, qd_out)[way].at[rows],
            dst_ref=q_in.at[source, rows],
            send_sem=q_send.at[c, dest],
            recv_sem=q_recv.at[c, source],
            device_id={"lay": dest},
            device_id_type=MESH,
        )

    def out_copy(c):
        rows = pl.ds(pl.multiple_of(c * QR, QR), QR)
        return pltpu.make_async_copy(res.at[:, rows, :], out_hbm.at[:, rows, :], out_sem.at[c])

    def ahead(way, k):
        return range(k + 1, NLAY) if way == 0 else range(k - 1, -1, -1)

    whole = (LINES, LANES)

    def to_steps(flat, steps_ref):
        for m in range(LINES // 8):
            for j in range(STEP):
                steps_ref[j, pl.ds(8 * m, 8), :] = flat[pl.ds(8 * STEP * m + j, 8, stride=STEP), :]

    def block_factors(steps_ref, w_ref, p_ref, r_ref):
        e = jnp.ones(whole, F32)
        r = jnp.ones(whole, F32)
        eb = jnp.ones(whole, F32)
        for j in range(1, STEP):
            s = steps_ref[j]
            se = s * e
            w = 1.0 / (1.0 + s + se)
            p = s * w
            e = (1.0 + se) * w
            r_now = r * p
            eb = eb - r * r_now
            r = r_now
            w_ref[j] = w
            p_ref[j] = p
            r_ref[j] = r
        return e, r, eb

    def e_stage(k):
        for way in range(2):

            @pl.when(lay == (k if way == 0 else NLAY - 1 - k))
            def _():
                me = k if way == 0 else NLAY - 1 - k
                src, out, wr, pr, prod = ((eu_in, eu_out, wu, pu, ru), (ed_in, ed_out, wd, pd, rd))[way]

                def step(c, carry):
                    rows = pl.ds(pl.multiple_of(c * ZR, ZR), ZR)
                    if k > 0:
                        e_copy(way, c, me).wait_recv()
                        e = src[rows, :]
                    else:
                        e = jnp.ones((ZR, LANES), F32)
                    total = None
                    for i in range(L) if way == 0 else range(L - 1, -1, -1):
                        s = ys[i, rows, :]
                        se = s * e
                        w = 1.0 / (1.0 + s + se)
                        e = (1.0 + se) * w
                        p = s * w
                        wr[i, rows, :] = w
                        pr[i, rows, :] = p
                        total = p if total is None else total * p
                    out[rows, :] = e
                    prod[rows, :] = total
                    if k < NLAY - 1:
                        e_copy(way, c, ahead(way, me)[0]).start()
                    return carry

                lax.fori_loop(0, ZCH, step, 0)

    loads = [
        pltpu.make_async_copy(zone_hbm, zone, in_sem.at[0]),
        pltpu.make_async_copy(flow_hbm, flow, in_sem.at[1]),
        pltpu.make_async_copy(fixed_hbm, fixed, in_sem.at[2]),
        pltpu.make_async_copy(sal_hbm, sal, in_sem.at[3]),
    ]
    for copy in loads:
        copy.start()

    barrier = pltpu.get_barrier_semaphore()

    def greet_col(o, carry):
        pl.semaphore_signal(barrier, inc=1, device_id={"col": (col + o) % NCOL}, device_id_type=MESH)
        return carry

    lax.fori_loop(1, NCOL, greet_col, 0)
    for o in range(1, NGRP):
        pl.semaphore_signal(barrier, inc=1, device_id={"grp": (grp + o) % NGRP}, device_id_type=MESH)
    for o in range(1, NLAY):
        pl.semaphore_signal(barrier, inc=1, device_id={"lay": (lay + o) % NLAY}, device_id_type=MESH)

    lane = lax.broadcasted_iota(jnp.int32, (8, LANES), 1)

    for copy in loads[:3]:
        copy.wait()
    table_long = [disp_ref[0, i] for i in range(8)]
    table_trans = [disp_ref[1, i] for i in range(8)]

    def couple(z, carry):
        for half in range(2):
            rows = pl.ds(8 * half, 8)
            for b in range(NCOL):
                cols = pl.ds(LANES * b, LANES)
                ids = zone[z, rows, cols]
                speed = flow[z, rows, cols]
                opened = 1.0 - fixed[z, rows, cols].astype(F32)
                st[b, z, rows, :] = opened * pick(ids, table_trans) * speed
                long_nat[b, z, rows, :] = opened * pick(ids, table_long) * speed
        return carry

    lax.fori_loop(0, L, couple, 0)

    pl.semaphore_wait(barrier, NCOL - 1 + NGRP - 1 + NLAY - 1)

    def s_start(o, carry):
        s_copy((col + o) % NCOL, col).start()
        return carry

    lax.fori_loop(1, NCOL, s_start, 0)
    ys[:, pl.ds(col * RB, RB), :] = st[col]

    to_steps(st.reshape(NCOL * LINES, LANES), yd)
    block_factors(yd, yw, yp, yr)

    loads[3].wait()

    def spread(z, carry):
        for half in range(2):
            rows = pl.ds(8 * half, 8)
            line = pl.ds(pl.multiple_of(z * RB + 8 * half, 8), 8)
            s_parts = butterfly([long_nat[b, z, rows, :] for b in range(NCOL)], lane)
            for j in range(STEP):
                us[j, line, :] = s_parts[j]
            f_parts = butterfly([sal[z, rows, pl.ds(LANES * b, LANES)] for b in range(NCOL)], lane)
            for j in range(STEP):
                uf[j, line, :] = f_parts[j]
        return carry

    lax.fori_loop(0, L, spread, 0)

    e = jnp.ones(whole, F32)
    r = jnp.ones(whole, F32)
    q = jnp.zeros(whole, F32)
    alpha = jnp.zeros(whole, F32)
    eb = jnp.ones(whole, F32)
    for j in range(1, STEP):
        s = us[j]
        f = uf[j]
        se = s * e
        w = 1.0 / (1.0 + s + se)
        p = s * w
        e = (1.0 + se) * w
        q = f * w + p * q
        r_now = r * p
        alpha = alpha + r * q
        eb = eb - r * r_now
        r = r_now
        up[j] = p
        uq[j] = q
        ur[j] = r

    lanes = lax.broadcasted_iota(jnp.int32, whole, 1)
    sub = lanes // 16
    low = lanes % 16
    first_block = lanes == 0
    last_block = lanes == LANES - 1

    def before(v, d):
        if d >= 8:
            return pltpu.roll(v, d // 8, 1)
        return jnp.where(sub >= d, pltpu.roll(v, 16 * d, 1), pltpu.roll(v, 16 * d + 1, 1))

    def after(v, d):
        if d >= 8:
            return pltpu.roll(v, LANES - d // 8, 1)
        return jnp.where(
            sub < 8 - d, pltpu.roll(v, LANES - 16 * d, 1), pltpu.roll(v, LANES - 16 * d - 1, 1)
        )

    s = us[0]
    ep_left = jnp.where(first_block, 1.0, before(e, 1))
    q_left = jnp.where(first_block, 0.0, before(q, 1))
    r_left = jnp.where(first_block, 0.0, before(r, 1))
    inv = 1.0 / (1.0 + s * (eb + ep_left))
    a = s * r_left * inv
    c = jnp.where(last_block, 0.0, s * r * inv)
    f = (uf[0] + s * (q_left + alpha)) * inv
    for m in range(7):
        d = 1 << m
        inv = 1.0 / (1.0 - a * before(c, d) - c * after(a, d))
        f = (f + a * before(f, d) + c * after(f, d)) * inv
        if m < 6:
            a, c = a * before(a, d) * inv, c * after(c, d) * inv

    uf[0] = f
    x = jnp.where(last_block, 0.0, after(f, 1))
    for j in range(STEP - 1, 0, -1):
        x = uq[j] + ur[j] * f + up[j] * x
        uf[j] = x

    def gather(z, carry):
        for half in range(2):
            rows = pl.ds(8 * half, 8)
            line = pl.ds(pl.multiple_of(z * RB + 8 * half, 8), 8)
            parts = butterfly([uf[j, line, :] for j in range(STEP)], lane)
            for b in range(NCOL):
                ft[b, z, rows, :] = parts[b]
        return carry

    lax.fori_loop(0, L, gather, 0)

    ft_flat = ft.reshape(NCOL * LINES, LANES)
    to_steps(ft_flat, yfd)
    q = yfd[1] * yw[1]
    yfd[1] = q
    alpha = q
    for j in range(2, STEP):
        q = yfd[j] * yw[j] + yp[j] * q
        yfd[j] = q
        alpha = alpha + yr[j - 1] * q
    head = yfd[0] + yd[0] * alpha
    for b in range(NCOL):
        ct[b, 0:L] = head[L * b : L * (b + 1)]
        ct[b, L : 2 * L] = q[L * b : L * (b + 1)]

    def c_start(o, carry):
        c_copy((col + o) % NCOL, col).start()
        return carry

    lax.fori_loop(1, NCOL, c_start, 0)
    cy[col] = ct[col]

    x = yfd[STEP - 1]
    for j in range(STEP - 1, -1, -1):
        if j == 0:
            x = jnp.zeros(whole, F32)
        elif j < STEP - 1:
            x = yfd[j] + yp[j] * x
        for m in range(LINES // 8):
            ft_flat[pl.ds(8 * STEP * m + j, 8, stride=STEP), :] = x[8 * m : 8 * m + 8]

    def f_start(o, carry):
        f_copy((col + o) % NCOL, col).start()
        return carry

    lax.fori_loop(1, NCOL, f_start, 0)
    yf[:, pl.ds(col * RB, RB), :] = ft[col]

    def s_wait(o, carry):
        s_copy(col, (col + NCOL - o) % NCOL).wait_recv()
        return carry

    lax.fori_loop(1, NCOL, s_wait, 0)

    to_steps(ys.reshape(L * ROWS, LANES), yd)

    e, r, eb = block_factors(yd, yw, yp, yr)
    block = lax.broadcasted_iota(jnp.int32, whole, 0) % RB

    def above(v, d, edge):
        return jnp.where(block >= d, pltpu.roll(v, d, 0), edge)

    def below(v, d, edge):
        return jnp.where(block < RB - d, pltpu.roll(v, LINES - d, 0), edge)

    s = yd[0]
    inv = 1.0 / (1.0 + s * (eb + above(e, 1, 1.0)))
    a = s * above(r, 1, 1.0) * inv
    c = s * r * inv
    yw[0] = inv
    for m in range(4):
        d = 1 << m
        inv = 1.0 / (1.0 - a * above(c, d, 0.0) - c * below(a, d, 0.0))
        lev_a[m] = a * inv
        lev_c[m] = c * inv
        lev_i[m] = inv
        a, c = a * above(a, d, 1.0) * inv, c * below(c, d, 1.0) * inv
    lev_a[4] = a
    lev_c[4] = c
    top = pl.ds(0, L, stride=RB)
    bottom = pl.ds(RB - 1, L, stride=RB)
    tmp[0] = r * a
    tmp[1] = (1.0 - e) + r * c
    gcoef[grp, 0 * L : 1 * L] = lev_a[4, top, :]
    gcoef[grp, 1 * L : 2 * L] = lev_c[4, top, :]
    gcoef[grp, 2 * L : 3 * L] = tmp[0, bottom, :]
    gcoef[grp, 3 * L : 4 * L] = tmp[1, bottom, :]

    for o in range(1, NGRP):
        g_copy(gcoef, gc_send, gc_recv, (grp + o) % NGRP, grp).start()

    e_stage(0)

    def c_wait(o, carry):
        c_copy(col, (col + NCOL - o) % NCOL).wait_recv()
        return carry

    lax.fori_loop(1, NCOL, c_wait, 0)
    for k in range(NCOL):
        tmp[2, pl.ds(k, L, stride=NCOL), :] = cy[k, 0:L]
        tmp[3, pl.ds(k, L, stride=NCOL), :] = cy[k, L : 2 * L]

    q = tmp[3]
    f = (tmp[2] + yd[0] * above(q, 1, 0.0)) * yw[0]
    for m in range(4):
        d = 1 << m
        f = f * lev_i[m] + lev_a[m] * above(f, d, 0.0) + lev_c[m] * below(f, d, 0.0)
    tmp[2] = f
    tmp[3] = q + yr[STEP - 1] * f
    gval[grp, 0 * L : 1 * L] = tmp[2, top, :]
    gval[grp, 1 * L : 2 * L] = tmp[3, bottom, :]

    for o in range(1, NGRP):
        g_copy(gval, gv_send, gv_recv, (grp + o) % NGRP, grp).start()

    to_left = jnp.zeros(whole, F32)
    to_right = jnp.ones(whole, F32)
    yb_flat = yb.reshape(L * ROWS, LANES)
    yc_flat = yc.reshape(L * ROWS, LANES)
    for j in range(STEP - 1, -1, -1):
        if j == 0:
            to_left, to_right = jnp.ones(whole, F32), jnp.zeros(whole, F32)
        else:
            to_left = yr[j] + yp[j] * to_left
            to_right = yp[j] * to_right
        for m in range(LINES // 8):
            rows = pl.ds(8 * STEP * m + j, 8, stride=STEP)
            yb_flat[rows, :] = to_left[8 * m : 8 * m + 8]
            yc_flat[rows, :] = to_right[8 * m : 8 * m + 8]

    e_stage(1)

    for o in range(1, NGRP):
        g_copy(gcoef, gc_send, gc_recv, grp, (grp + NGRP - o) % NGRP).wait_recv()
    for o in range(1, NGRP):
        g_copy(gval, gv_send, gv_recv, grp, (grp + NGRP - o) % NGRP).wait_recv()

    be = [gcoef[g, 0 * L : 1 * L] for g in range(NGRP)]
    ga = [gcoef[g, 1 * L : 2 * L] for g in range(NGRP)]
    rr = [gcoef[g, 2 * L : 3 * L] for g in range(NGRP)]
    pp = [gcoef[g, 3 * L : 4 * L] for g in range(NGRP)]
    al = [gval[g, 0 * L : 1 * L] for g in range(NGRP)]
    qq = [gval[g, 1 * L : 2 * L] for g in range(NGRP)]
    pre_p, pre_q = [pp[0]], [qq[0]]
    for g in range(1, NGRP - 1):
        t = rr[g] / (1.0 - pre_p[-1] * be[g])
        pre_p, pre_q = (
            pre_p + [pp[g] + t * pre_p[-1] * ga[g]],
            pre_q + [qq[g] + t * (pre_q[-1] + pre_p[-1] * al[g])],
        )
    suf_p, suf_q = [be[NGRP - 1]], [al[NGRP - 1]]
    for g in range(NGRP - 2, 0, -1):
        t = ga[g] * suf_p[0] / (1.0 - pp[g] * suf_p[0])
        suf_p, suf_q = (
            [be[g] + t * rr[g]] + suf_p,
            [al[g] + ga[g] * suf_q[0] + t * (qq[g] + pp[g] * suf_q[0])] + suf_q,
        )
    left = jnp.zeros((L, LANES), F32)
    right = jnp.zeros((L, LANES), F32)
    for i in range(NGRP - 1):
        u = (pre_q[i] + pre_p[i] * suf_q[i]) / (1.0 - pre_p[i] * suf_p[i])
        v = suf_q[i] + suf_p[i] * u
        left = jnp.where(grp == i + 1, u, left)
        right = jnp.where(grp == i, v, right)

    def per_line(v):
        return jnp.concatenate([jnp.broadcast_to(v[z : z + 1], (RB, LANES)) for z in range(L)], 0)

    right = per_line(right)
    f = f + lev_a[4] * per_line(left) + lev_c[4] * right
    tmp[2] = f
    tmp[3] = jnp.where(block == RB - 1, right, pltpu.roll(f, LINES - 1, 0))

    def f_wait(o, carry):
        f_copy(col, (col + NCOL - o) % NCOL).wait_recv()
        return carry

    lax.fori_loop(1, NCOL, f_wait, 0)

    def fill(c):
        for z in range(L):
            for n in range(QR // RB):
                rows = pl.ds(pl.multiple_of(c * QR + RB * n, RB), RB)
                line = pl.ds(z * NCOL + c * (QR // RB) + n, 1)
                sec[z, rows, :] = yf[z, rows, :] + yb[z, rows, :] * tmp[2, line, :] + yc[z, rows, :] * tmp[3, line, :]

    def q_pass(k, way, back):
        out, wr, pr = ((qu_out, wu, pu), (qd_out, wd, pd))[way]
        order = list(range(L) if way == 0 else range(L - 1, -1, -1))
        behind = k - 1 if way == 0 else k + 1

        def step(c, carry):
            rows = pl.ds(pl.multiple_of(c * QR, QR), QR)
            if back < 2:
                fill(c)
            if back > 0:
                q_copy(0, c, k, behind).wait_recv()
                q = q_in[behind, rows, :]
            for i in order:
                mine = sec[i, rows, :] * wr[i, rows, :]
                q = mine if (back == 0 and i == order[0]) else mine + pr[i, rows, :] * q
            out[rows, :] = q
            q_copy(way, c, ahead(way, k)[0], k).start()
            return carry

        lax.fori_loop(0, QCH, step, 0)

    for k, way, back in ((0, 0, 0), (1, 0, 1), (2, 1, 1), (3, 1, 0)):

        @pl.when(lay == k)
        def _():
            q_pass(k, way, back)

    e_stage(2)
    for k, way in ((1, 1), (2, 0)):

        @pl.when(lay == k)
        def _():
            q_pass(k, way, 2)

    e_stage(3)

    for k in range(NLAY):

        @pl.when(lay == k)
        def _():
            below_from = {0: None, 1: 0, 2: 1, 3: 2}[k]
            above_from = {0: 1, 1: 2, 2: 3, 3: None}[k]

            def finish(c, carry):
                rows = pl.ds(pl.multiple_of(c * QR, QR), QR)
                if k in (0, NLAY - 1):
                    q_copy(0, c, k, 1 if k == 0 else 2).wait_recv()
                q = None if below_from is None else q_in[below_from, rows, :]
                q_all = []
                for i in range(L):
                    mine = sec[i, rows, :] * wu[i, rows, :]
                    q = mine if q is None else mine + pu[i, rows, :] * q
                    q_all.append(q)
                x = q
                if above_from is not None:
                    ep = eu_out[rows, :]
                    p = 1.0 - ep
                    x = (q + p * q_in[above_from, rows, :]) / (ep + p * ed_in[rows, :])
                out_hbm[L - 1, rows, :] = x
                for i in range(L - 2, -1, -1):
                    x = q_all[i] + pu[i, rows, :] * x
                    out_hbm[i, rows, :] = x
                return carry

            lax.fori_loop(0, QCH, finish, 0)

    def s_done(o, carry):
        s_copy((col + o) % NCOL, col).wait_send()
        c_copy((col + o) % NCOL, col).wait_send()
        f_copy((col + o) % NCOL, col).wait_send()
        return carry

    lax.fori_loop(1, NCOL, s_done, 0)
    for o in range(1, NGRP):
        g_copy(gcoef, gc_send, gc_recv, (grp + o) % NGRP, grp).wait_send()
        g_copy(gval, gv_send, gv_recv, (grp + o) % NGRP, grp).wait_send()
    for k in range(NLAY):

        @pl.when(lay == k)
        def _():
            for way in range(2):
                back = k if way == 0 else NLAY - 1 - k
                if back == NLAY - 1:
                    continue
                dest = ahead(way, k)[0]
                for c in range(ZCH):
                    e_copy(way, c, dest).wait_send()
                for c in range(QCH):
                    q_copy(way, c, dest, k).wait_send()


def per_device(salinity, zone_ids, flow_speed, fixed_cells, dispersivity):
    hbm = pl.BlockSpec(memory_space=pl.ANY)
    fixed = pl.BlockSpec(memory_space=pltpu.HBM)
    nat = (L, RB, NCOL * LANES)
    slab = (L, ROWS, LANES)
    by_dest = (NCOL, L, RB, LANES)
    steps = (STEP, LINES, LANES)
    plane = (ROWS, LANES)

    def vm(shape, dtype=F32):
        return pltpu.VMEM(shape, dtype)

    dma = pltpu.SemaphoreType.DMA
    return pl.pallas_call(
        kernel,
        out_shape=jax.ShapeDtypeStruct(slab, F32),
        in_specs=[hbm, hbm, hbm, hbm, pl.BlockSpec(memory_space=pltpu.SMEM)],
        out_specs=pl.BlockSpec(memory_space=pltpu.VMEM),
        scratch_shapes=[
            vm(nat), vm(nat, jnp.int32), vm(nat), vm(nat, jnp.int32),
            vm(by_dest), vm(by_dest), vm(by_dest), vm((NCOL, 2 * L, LANES)), vm(slab), vm(slab),
            vm((NCOL, 2 * L, LANES)), vm(slab), vm(slab),
            vm(steps), vm(steps), vm(steps), vm(steps), vm(steps),
            vm(steps), vm(steps), vm(steps), vm(steps), vm(steps),
            vm((5, LINES, LANES)), vm((5, LINES, LANES)), vm((4, LINES, LANES)), vm((4, LINES, LANES)),
            vm((NGRP, 4 * L, LANES)), vm((NGRP, 2 * L, LANES)),
            vm(slab), vm(slab), vm(slab), vm(slab), vm(slab),
            vm(plane), vm(plane), vm(plane), vm(plane), vm(plane), vm(plane), vm(plane),
            vm(plane), vm(plane), vm((NLAY,) + plane), vm(slab),
            dma((4,)), dma((NCOL,)), dma((NCOL,)), dma((NCOL,)), dma((NCOL,)), dma((NCOL,)), dma((NCOL,)),
            dma((NGRP,)), dma((NGRP,)), dma((NGRP,)), dma((NGRP,)),
            dma((2, ZCH)), dma((2, ZCH)), dma((1,)), dma((1,)), dma((QCH, NLAY)), dma((QCH, NLAY)), dma((QCH,)),
        ],
        compiler_params=pltpu.CompilerParams(
            collective_id=0, has_side_effects=True, vmem_limit_bytes=54272 * 1024
        ),
        name="lod_step",
    )(salinity, zone_ids, flow_speed, fixed_cells, dispersivity)


def solution(mesh):
    placed = P("lay", ("grp", "col"), None)
    return jax.shard_map(
        per_device,
        mesh=mesh,
        in_specs=(placed, placed, placed, placed, P()),
        out_specs=P("lay", "grp", "col"),
        check_vma=False,
    )
```

```python
import jax
import jax.numpy as jnp
from jax import lax
from jax.experimental import pallas as pl
from jax.experimental.pallas import tpu as pltpu
from jax.sharding import PartitionSpec as P

NCOL = 16
NGRP = 4
NLAY = 4
L = 4
RB = 16
LINES = L * RB
LANES = 128
STEP = 16
ROWS = NCOL * RB
ZCH = 4
ZR = ROWS // ZCH
QCH = 4
QR = ROWS // QCH
MESH = pl.DeviceIdType.MESH
F32 = jnp.float32


def butterfly(parts, lane):
    parts = list(parts)
    for m in range(4):
        step = 1 << m
        high = (lane & step) != 0
        for i in range(16):
            if i & step:
                continue
            a, b = parts[i], parts[i + step]
            parts[i] = jnp.where(high, pltpu.roll(b, step, 1), a)
            parts[i + step] = jnp.where(high, b, pltpu.roll(a, LANES - step, 1))
    return parts


def pick(zone, table):
    for m in range(3):
        bit = (zone & (1 << m)) != 0
        table = [jnp.where(bit, table[i + 1], table[i]) for i in range(0, len(table), 2)]
    return table[0]


def kernel(
    sal_hbm, zone_hbm, flow_hbm, fixed_hbm, disp_ref, out_hbm,
    sal, zone, flow, fixed,
    long_nat, st, ft, ct, ys, yf, cy, yb, yc,
    us, uf, up, uq, ur,
    yd, yfd, yp, yw, yr, lev_a, lev_c, lev_i, tmp,
    gcoef, gval,
    sec, wu, pu, wd, pd, eu_in, ed_in, eu_out, ed_out, ru, rd, r_in, qu_out, qd_out, q_in, res,
    in_sem, s_send, s_recv, c_send, c_recv, f_send, f_recv, gc_send, gc_recv, gv_send, gv_recv,
    e_send, e_recv, r_send, r_recv, q_send, q_recv, out_sem,
):
    grp = lax.axis_index("grp")
    col = lax.axis_index("col")
    lay = lax.axis_index("lay")

    def partner(m):
        return ((col // 4 + (4 - m // 4) % 4) % 4) * 4 + (col % 4 + m % 4) % 4

    def s_copy(dest, source):
        return pltpu.make_async_remote_copy(
            src_ref=st.at[dest],
            dst_ref=ys.at[:, pl.ds(source * RB, RB), :],
            send_sem=s_send.at[dest],
            recv_sem=s_recv.at[source],
            device_id={"col": dest},
            device_id_type=MESH,
        )

    def f_copy(dest, source):
        return pltpu.make_async_remote_copy(
            src_ref=ft.at[dest],
            dst_ref=yf.at[:, pl.ds(source * RB, RB), :],
            send_sem=f_send.at[dest],
            recv_sem=f_recv.at[source],
            device_id={"col": dest},
            device_id_type=MESH,
        )

    def c_copy(dest, source):
        return pltpu.make_async_remote_copy(
            src_ref=ct.at[dest],
            dst_ref=cy.at[source],
            send_sem=c_send.at[dest],
            recv_sem=c_recv.at[source],
            device_id={"col": dest},
            device_id_type=MESH,
        )

    def g_copy(buf, send, recv, dest, source):
        return pltpu.make_async_remote_copy(
            src_ref=buf.at[source],
            dst_ref=buf.at[source],
            send_sem=send.at[dest],
            recv_sem=recv.at[source],
            device_id={"grp": dest},
            device_id_type=MESH,
        )

    def e_copy(way, c, dest):
        rows = pl.ds(pl.multiple_of(c * ZR, ZR), ZR)
        src, dst = ((eu_out, eu_in), (ed_out, ed_in))[way]
        return pltpu.make_async_remote_copy(
            src_ref=src.at[rows],
            dst_ref=dst.at[rows],
            send_sem=e_send.at[way, c],
            recv_sem=e_recv.at[way, c],
            device_id={"lay": dest},
            device_id_type=MESH,
        )

    def r_copy(way, dest):
        return pltpu.make_async_remote_copy(
            src_ref=(ru, rd)[way],
            dst_ref=r_in,
            send_sem=r_send.at[0],
            recv_sem=r_recv.at[0],
            device_id={"lay": dest},
            device_id_type=MESH,
        )

    def q_copy(way, c, dest, source):
        rows = pl.ds(pl.multiple_of(c * QR, QR), QR)
        return pltpu.make_async_remote_copy(
            src_ref=(qu_out, qd_out)[way].at[rows],
            dst_ref=q_in.at[source, rows],
            send_sem=q_send.at[c, dest],
            recv_sem=q_recv.at[c, source],
            device_id={"lay": dest},
            device_id_type=MESH,
        )

    def out_copy(c):
        rows = pl.ds(pl.multiple_of(c * QR, QR), QR)
        return pltpu.make_async_copy(res.at[:, rows, :], out_hbm.at[:, rows, :], out_sem.at[c])

    def ahead(way, k):
        return range(k + 1, NLAY) if way == 0 else range(k - 1, -1, -1)

    whole = (LINES, LANES)

    def to_steps(flat, steps_ref):
        for m in range(LINES // 8):
            for j in range(STEP):
                steps_ref[j, pl.ds(8 * m, 8), :] = flat[pl.ds(8 * STEP * m + j, 8, stride=STEP), :]

    def block_factors(steps_ref, w_ref, p_ref, r_ref):
        e = jnp.ones(whole, F32)
        r = jnp.ones(whole, F32)
        eb = jnp.ones(whole, F32)
        for j in range(1, STEP):
            s = steps_ref[j]
            se = s * e
            w = 1.0 / (1.0 + s + se)
            p = s * w
            e = (1.0 + se) * w
            r_now = r * p
            eb = eb - r * r_now
            r = r_now
            w_ref[j] = w
            p_ref[j] = p
            r_ref[j] = r
        return e, r, eb

    def e_stage(k):
        for way in range(2):

            @pl.when(lay == (k if way == 0 else NLAY - 1 - k))
            def _():
                me = k if way == 0 else NLAY - 1 - k
                src, out, wr, pr, prod = ((eu_in, eu_out, wu, pu, ru), (ed_in, ed_out, wd, pd, rd))[way]

                def step(c, carry):
                    rows = pl.ds(pl.multiple_of(c * ZR, ZR), ZR)
                    if k > 0:
                        e_copy(way, c, me).wait_recv()
                        e = src[rows, :]
                    else:
                        e = jnp.ones((ZR, LANES), F32)
                    total = None
                    for i in range(L) if way == 0 else range(L - 1, -1, -1):
                        s = ys[i, rows, :]
                        se = s * e
                        w = 1.0 / (1.0 + s + se)
                        e = (1.0 + se) * w
                        p = s * w
                        wr[i, rows, :] = w
                        pr[i, rows, :] = p
                        total = p if total is None else total * p
                    out[rows, :] = e
                    prod[rows, :] = total
                    if k < NLAY - 1:
                        e_copy(way, c, ahead(way, me)[0]).start()
                    return carry

                lax.fori_loop(0, ZCH, step, 0)

    loads = [
        pltpu.make_async_copy(zone_hbm, zone, in_sem.at[0]),
        pltpu.make_async_copy(flow_hbm, flow, in_sem.at[1]),
        pltpu.make_async_copy(fixed_hbm, fixed, in_sem.at[2]),
        pltpu.make_async_copy(sal_hbm, sal, in_sem.at[3]),
    ]
    for copy in loads:
        copy.start()

    barrier = pltpu.get_barrier_semaphore()

    def greet_col(o, carry):
        pl.semaphore_signal(barrier, inc=1, device_id={"col": (col + o) % NCOL}, device_id_type=MESH)
        return carry

    lax.fori_loop(1, NCOL, greet_col, 0)
    for o in range(1, NGRP):
        pl.semaphore_signal(barrier, inc=1, device_id={"grp": (grp + o) % NGRP}, device_id_type=MESH)
    for o in range(1, NLAY):
        pl.semaphore_signal(barrier, inc=1, device_id={"lay": (lay + o) % NLAY}, device_id_type=MESH)

    lane = lax.broadcasted_iota(jnp.int32, (8, LANES), 1)

    for copy in loads[:3]:
        copy.wait()
    table_long = [disp_ref[0, i] for i in range(8)]
    table_trans = [disp_ref[1, i] for i in range(8)]

    def couple(z, carry):
        for half in range(2):
            rows = pl.ds(8 * half, 8)
            for b in range(NCOL):
                cols = pl.ds(LANES * b, LANES)
                ids = zone[z, rows, cols]
                speed = flow[z, rows, cols]
                opened = 1.0 - fixed[z, rows, cols].astype(F32)
                st[b, z, rows, :] = opened * pick(ids, table_trans) * speed
                long_nat[b, z, rows, :] = opened * pick(ids, table_long) * speed
        return carry

    lax.fori_loop(0, L, couple, 0)

    pl.semaphore_wait(barrier, NCOL - 1 + NGRP - 1 + NLAY - 1)

    def s_start(o, carry):
        s_copy(partner(o), col).start()
        return carry

    lax.fori_loop(1, NCOL, s_start, 0)
    ys[:, pl.ds(col * RB, RB), :] = st[col]

    to_steps(st.reshape(NCOL * LINES, LANES), yd)
    block_factors(yd, yw, yp, yr)

    loads[3].wait()

    def spread(z, carry):
        for half in range(2):
            rows = pl.ds(8 * half, 8)
            line = pl.ds(pl.multiple_of(z * RB + 8 * half, 8), 8)
            s_parts = butterfly([long_nat[b, z, rows, :] for b in range(NCOL)], lane)
            for j in range(STEP):
                us[j, line, :] = s_parts[j]
            f_parts = butterfly([sal[z, rows, pl.ds(LANES * b, LANES)] for b in range(NCOL)], lane)
            for j in range(STEP):
                uf[j, line, :] = f_parts[j]
        return carry

    lax.fori_loop(0, L, spread, 0)

    e = jnp.ones(whole, F32)
    r = jnp.ones(whole, F32)
    q = jnp.zeros(whole, F32)
    alpha = jnp.zeros(whole, F32)
    eb = jnp.ones(whole, F32)
    for j in range(1, STEP):
        s = us[j]
        f = uf[j]
        se = s * e
        w = 1.0 / (1.0 + s + se)
        p = s * w
        e = (1.0 + se) * w
        q = f * w + p * q
        r_now = r * p
        alpha = alpha + r * q
        eb = eb - r * r_now
        r = r_now
        up[j] = p
        uq[j] = q
        ur[j] = r

    lanes = lax.broadcasted_iota(jnp.int32, whole, 1)
    sub = lanes // 16
    low = lanes % 16
    first_block = lanes == 0
    last_block = lanes == LANES - 1

    def before(v, d):
        if d >= 8:
            return pltpu.roll(v, d // 8, 1)
        return jnp.where(sub >= d, pltpu.roll(v, 16 * d, 1), pltpu.roll(v, 16 * d + 1, 1))

    def after(v, d):
        if d >= 8:
            return pltpu.roll(v, LANES - d // 8, 1)
        return jnp.where(
            sub < 8 - d, pltpu.roll(v, LANES - 16 * d, 1), pltpu.roll(v, LANES - 16 * d - 1, 1)
        )

    s = us[0]
    ep_left = jnp.where(first_block, 1.0, before(e, 1))
    q_left = jnp.where(first_block, 0.0, before(q, 1))
    r_left = jnp.where(first_block, 0.0, before(r, 1))
    inv = 1.0 / (1.0 + s * (eb + ep_left))
    a = s * r_left * inv
    c = jnp.where(last_block, 0.0, s * r * inv)
    f = (uf[0] + s * (q_left + alpha)) * inv
    for m in range(7):
        d = 1 << m
        inv = 1.0 / (1.0 - a * before(c, d) - c * after(a, d))
        f = (f + a * before(f, d) + c * after(f, d)) * inv
        if m < 6:
            a, c = a * before(a, d) * inv, c * after(c, d) * inv

    uf[0] = f
    x = jnp.where(last_block, 0.0, after(f, 1))
    for j in range(STEP - 1, 0, -1):
        x = uq[j] + ur[j] * f + up[j] * x
        uf[j] = x

    def gather(z, carry):
        for half in range(2):
            rows = pl.ds(8 * half, 8)
            line = pl.ds(pl.multiple_of(z * RB + 8 * half, 8), 8)
            parts = butterfly([uf[j, line, :] for j in range(STEP)], lane)
            for b in range(NCOL):
                ft[b, z, rows, :] = parts[b]
        return carry

    lax.fori_loop(0, L, gather, 0)

    ft_flat = ft.reshape(NCOL * LINES, LANES)
    to_steps(ft_flat, yfd)
    q = yfd[1] * yw[1]
    yfd[1] = q
    alpha = q
    for j in range(2, STEP):
        q = yfd[j] * yw[j] + yp[j] * q
        yfd[j] = q
        alpha = alpha + yr[j - 1] * q
    head = yfd[0] + yd[0] * alpha
    for b in range(NCOL):
        ct[b, 0:L] = head[L * b : L * (b + 1)]
        ct[b, L : 2 * L] = q[L * b : L * (b + 1)]

    def c_start(o, carry):
        c_copy(partner(o), col).start()
        return carry

    lax.fori_loop(1, NCOL, c_start, 0)
    cy[col] = ct[col]

    x = yfd[STEP - 1]
    for j in range(STEP - 1, -1, -1):
        if j == 0:
            x = jnp.zeros(whole, F32)
        elif j < STEP - 1:
            x = yfd[j] + yp[j] * x
        for m in range(LINES // 8):
            ft_flat[pl.ds(8 * STEP * m + j, 8, stride=STEP), :] = x[8 * m : 8 * m + 8]

    def f_start(o, carry):
        f_copy(partner(o), col).start()
        return carry

    lax.fori_loop(1, NCOL, f_start, 0)
    yf[:, pl.ds(col * RB, RB), :] = ft[col]

    def s_wait(o, carry):
        s_copy(col, (col + NCOL - o) % NCOL).wait_recv()
        return carry

    lax.fori_loop(1, NCOL, s_wait, 0)

    to_steps(ys.reshape(L * ROWS, LANES), yd)

    e, r, eb = block_factors(yd, yw, yp, yr)
    block = lax.broadcasted_iota(jnp.int32, whole, 0) % RB

    def above(v, d, edge):
        return jnp.where(block >= d, pltpu.roll(v, d, 0), edge)

    def below(v, d, edge):
        return jnp.where(block < RB - d, pltpu.roll(v, LINES - d, 0), edge)

    s = yd[0]
    inv = 1.0 / (1.0 + s * (eb + above(e, 1, 1.0)))
    a = s * above(r, 1, 1.0) * inv
    c = s * r * inv
    yw[0] = inv
    for m in range(4):
        d = 1 << m
        inv = 1.0 / (1.0 - a * above(c, d, 0.0) - c * below(a, d, 0.0))
        lev_a[m] = a * inv
        lev_c[m] = c * inv
        lev_i[m] = inv
        a, c = a * above(a, d, 1.0) * inv, c * below(c, d, 1.0) * inv
    lev_a[4] = a
    lev_c[4] = c
    top = pl.ds(0, L, stride=RB)
    bottom = pl.ds(RB - 1, L, stride=RB)
    tmp[0] = r * a
    tmp[1] = (1.0 - e) + r * c
    gcoef[grp, 0 * L : 1 * L] = lev_a[4, top, :]
    gcoef[grp, 1 * L : 2 * L] = lev_c[4, top, :]
    gcoef[grp, 2 * L : 3 * L] = tmp[0, bottom, :]
    gcoef[grp, 3 * L : 4 * L] = tmp[1, bottom, :]

    for o in range(1, NGRP):
        g_copy(gcoef, gc_send, gc_recv, (grp + o) % NGRP, grp).start()

    def c_wait(o, carry):
        c_copy(col, (col + NCOL - o) % NCOL).wait_recv()
        return carry

    lax.fori_loop(1, NCOL, c_wait, 0)
    for k in range(NCOL):
        tmp[2, pl.ds(k, L, stride=NCOL), :] = cy[k, 0:L]
        tmp[3, pl.ds(k, L, stride=NCOL), :] = cy[k, L : 2 * L]

    q = tmp[3]
    f = (tmp[2] + yd[0] * above(q, 1, 0.0)) * yw[0]
    for m in range(4):
        d = 1 << m
        f = f * lev_i[m] + lev_a[m] * above(f, d, 0.0) + lev_c[m] * below(f, d, 0.0)
    tmp[2] = f
    tmp[3] = q + yr[STEP - 1] * f
    gval[grp, 0 * L : 1 * L] = tmp[2, top, :]
    gval[grp, 1 * L : 2 * L] = tmp[3, bottom, :]

    for o in range(1, NGRP):
        g_copy(gval, gv_send, gv_recv, (grp + o) % NGRP, grp).start()

    e_stage(0)

    to_left = jnp.zeros(whole, F32)
    to_right = jnp.ones(whole, F32)
    yb_flat = yb.reshape(L * ROWS, LANES)
    yc_flat = yc.reshape(L * ROWS, LANES)
    for j in range(STEP - 1, -1, -1):
        if j == 0:
            to_left, to_right = jnp.ones(whole, F32), jnp.zeros(whole, F32)
        else:
            to_left = yr[j] + yp[j] * to_left
            to_right = yp[j] * to_right
        for m in range(LINES // 8):
            rows = pl.ds(8 * STEP * m + j, 8, stride=STEP)
            yb_flat[rows, :] = to_left[8 * m : 8 * m + 8]
            yc_flat[rows, :] = to_right[8 * m : 8 * m + 8]

    e_stage(1)

    for o in range(1, NGRP):
        g_copy(gcoef, gc_send, gc_recv, grp, (grp + NGRP - o) % NGRP).wait_recv()
    for o in range(1, NGRP):
        g_copy(gval, gv_send, gv_recv, grp, (grp + NGRP - o) % NGRP).wait_recv()

    be = [gcoef[g, 0 * L : 1 * L] for g in range(NGRP)]
    ga = [gcoef[g, 1 * L : 2 * L] for g in range(NGRP)]
    rr = [gcoef[g, 2 * L : 3 * L] for g in range(NGRP)]
    pp = [gcoef[g, 3 * L : 4 * L] for g in range(NGRP)]
    al = [gval[g, 0 * L : 1 * L] for g in range(NGRP)]
    qq = [gval[g, 1 * L : 2 * L] for g in range(NGRP)]
    pre_p, pre_q = [pp[0]], [qq[0]]
    for g in range(1, NGRP - 1):
        t = rr[g] / (1.0 - pre_p[-1] * be[g])
        pre_p, pre_q = (
            pre_p + [pp[g] + t * pre_p[-1] * ga[g]],
            pre_q + [qq[g] + t * (pre_q[-1] + pre_p[-1] * al[g])],
        )
    suf_p, suf_q = [be[NGRP - 1]], [al[NGRP - 1]]
    for g in range(NGRP - 2, 0, -1):
        t = ga[g] * suf_p[0] / (1.0 - pp[g] * suf_p[0])
        suf_p, suf_q = (
            [be[g] + t * rr[g]] + suf_p,
            [al[g] + ga[g] * suf_q[0] + t * (qq[g] + pp[g] * suf_q[0])] + suf_q,
        )
    left = jnp.zeros((L, LANES), F32)
    right = jnp.zeros((L, LANES), F32)
    for i in range(NGRP - 1):
        u = (pre_q[i] + pre_p[i] * suf_q[i]) / (1.0 - pre_p[i] * suf_p[i])
        v = suf_q[i] + suf_p[i] * u
        left = jnp.where(grp == i + 1, u, left)
        right = jnp.where(grp == i, v, right)

    def per_line(v):
        return jnp.concatenate([jnp.broadcast_to(v[z : z + 1], (RB, LANES)) for z in range(L)], 0)

    right = per_line(right)
    f = f + lev_a[4] * per_line(left) + lev_c[4] * right
    tmp[2] = f
    tmp[3] = jnp.where(block == RB - 1, right, pltpu.roll(f, LINES - 1, 0))


    def fill(c):
        for n in range(QR // RB):
            source = c * (QR // RB) + n

            @pl.when(source != col)
            def _():
                f_copy(col, source).wait_recv()

        for z in range(L):
            for n in range(QR // RB):
                rows = pl.ds(pl.multiple_of(c * QR + RB * n, RB), RB)
                line = pl.ds(z * NCOL + c * (QR // RB) + n, 1)
                sec[z, rows, :] = yf[z, rows, :] + yb[z, rows, :] * tmp[2, line, :] + yc[z, rows, :] * tmp[3, line, :]

    def q_pass(k, way, back):
        out, wr, pr = ((qu_out, wu, pu), (qd_out, wd, pd))[way]
        order = list(range(L) if way == 0 else range(L - 1, -1, -1))
        behind = k - 1 if way == 0 else k + 1

        def step(i, carry):
            c = (i + col // 4) % QCH
            rows = pl.ds(pl.multiple_of(c * QR, QR), QR)
            if back < 2:
                fill(c)
            if back > 0:
                q_copy(0, c, k, behind).wait_recv()
                q = q_in[behind, rows, :]
            for i in order:
                mine = sec[i, rows, :] * wr[i, rows, :]
                q = mine if (back == 0 and i == order[0]) else mine + pr[i, rows, :] * q
            out[rows, :] = q
            q_copy(way, c, ahead(way, k)[0], k).start()
            return carry

        lax.fori_loop(0, QCH, step, 0)

    for k, way, back in ((0, 0, 0), (1, 0, 1), (2, 1, 1), (3, 1, 0)):

        @pl.when(lay == k)
        def _():
            q_pass(k, way, back)

    e_stage(2)
    for k, way in ((1, 1), (2, 0)):

        @pl.when(lay == k)
        def _():
            q_pass(k, way, 2)

    e_stage(3)

    for k in range(NLAY):

        @pl.when(lay == k)
        def _():
            below_from = {0: None, 1: 0, 2: 1, 3: 2}[k]
            above_from = {0: 1, 1: 2, 2: 3, 3: None}[k]

            def finish(i, carry):
                c = (i + col // 4) % QCH
                rows = pl.ds(pl.multiple_of(c * QR, QR), QR)
                if k in (0, NLAY - 1):
                    q_copy(0, c, k, 1 if k == 0 else 2).wait_recv()
                q = None if below_from is None else q_in[below_from, rows, :]
                q_all = []
                for i in range(L):
                    mine = sec[i, rows, :] * wu[i, rows, :]
                    q = mine if q is None else mine + pu[i, rows, :] * q
                    q_all.append(q)
                x = q
                if above_from is not None:
                    ep = eu_out[rows, :]
                    p = 1.0 - ep
                    x = (q + p * q_in[above_from, rows, :]) / (ep + p * ed_in[rows, :])
                out_hbm[L - 1, rows, :] = x
                for i in range(L - 2, -1, -1):
                    x = q_all[i] + pu[i, rows, :] * x
                    out_hbm[i, rows, :] = x
                return carry

            lax.fori_loop(0, QCH, finish, 0)

    def s_done(o, carry):
        s_copy((col + o) % NCOL, col).wait_send()
        c_copy((col + o) % NCOL, col).wait_send()
        f_copy((col + o) % NCOL, col).wait_send()
        return carry

    lax.fori_loop(1, NCOL, s_done, 0)
    for o in range(1, NGRP):
        g_copy(gcoef, gc_send, gc_recv, (grp + o) % NGRP, grp).wait_send()
        g_copy(gval, gv_send, gv_recv, (grp + o) % NGRP, grp).wait_send()
    for k in range(NLAY):

        @pl.when(lay == k)
        def _():
            for way in range(2):
                back = k if way == 0 else NLAY - 1 - k
                if back == NLAY - 1:
                    continue
                dest = ahead(way, k)[0]
                for c in range(ZCH):
                    e_copy(way, c, dest).wait_send()
                for c in range(QCH):
                    q_copy(way, c, dest, k).wait_send()


def per_device(salinity, zone_ids, flow_speed, fixed_cells, dispersivity):
    hbm = pl.BlockSpec(memory_space=pl.ANY)
    fixed = pl.BlockSpec(memory_space=pltpu.HBM)
    nat = (L, RB, NCOL * LANES)
    slab = (L, ROWS, LANES)
    by_dest = (NCOL, L, RB, LANES)
    steps = (STEP, LINES, LANES)
    plane = (ROWS, LANES)

    def vm(shape, dtype=F32):
        return pltpu.VMEM(shape, dtype)

    dma = pltpu.SemaphoreType.DMA
    return pl.pallas_call(
        kernel,
        out_shape=jax.ShapeDtypeStruct(slab, F32),
        in_specs=[hbm, hbm, hbm, hbm, pl.BlockSpec(memory_space=pltpu.SMEM)],
        out_specs=pl.BlockSpec(memory_space=pltpu.VMEM),
        scratch_shapes=[
            vm(nat), vm(nat, jnp.int32), vm(nat), vm(nat, jnp.int32),
            vm(by_dest), vm(by_dest), vm(by_dest), vm((NCOL, 2 * L, LANES)), vm(slab), vm(slab),
            vm((NCOL, 2 * L, LANES)), vm(slab), vm(slab),
            vm(steps), vm(steps), vm(steps), vm(steps), vm(steps),
            vm(steps), vm(steps), vm(steps), vm(steps), vm(steps),
            vm((5, LINES, LANES)), vm((5, LINES, LANES)), vm((4, LINES, LANES)), vm((4, LINES, LANES)),
            vm((NGRP, 4 * L, LANES)), vm((NGRP, 2 * L, LANES)),
            vm(slab), vm(slab), vm(slab), vm(slab), vm(slab),
            vm(plane), vm(plane), vm(plane), vm(plane), vm(plane), vm(plane), vm(plane),
            vm(plane), vm(plane), vm((NLAY,) + plane), vm(slab),
            dma((4,)), dma((NCOL,)), dma((NCOL,)), dma((NCOL,)), dma((NCOL,)), dma((NCOL,)), dma((NCOL,)),
            dma((NGRP,)), dma((NGRP,)), dma((NGRP,)), dma((NGRP,)),
            dma((2, ZCH)), dma((2, ZCH)), dma((1,)), dma((1,)), dma((QCH, NLAY)), dma((QCH, NLAY)), dma((QCH,)),
        ],
        compiler_params=pltpu.CompilerParams(
            collective_id=0, has_side_effects=True, vmem_limit_bytes=54272 * 1024
        ),
        name="lod_step",
    )(salinity, zone_ids, flow_speed, fixed_cells, dispersivity)


def solution(mesh):
    placed = P("lay", ("grp", "col"), None)
    return jax.shard_map(
        per_device,
        mesh=mesh,
        in_specs=(placed, placed, placed, placed, P()),
        out_specs=P("lay", "grp", "col"),
        check_vma=False,
    )
```

```python
import jax
import jax.numpy as jnp
from jax import lax
from jax.experimental import pallas as pl
from jax.experimental.pallas import tpu as pltpu
from jax.sharding import PartitionSpec as P

NCOL = 16
NGRP = 4
NLAY = 4
L = 4
RB = 16
LINES = L * RB
LANES = 128
STEP = 16
ROWS = NCOL * RB
ZCH = 4
ZR = ROWS // ZCH
QCH = 4
QR = ROWS // QCH
MESH = pl.DeviceIdType.MESH
F32 = jnp.float32


def butterfly(parts, lane):
    parts = list(parts)
    for m in range(4):
        step = 1 << m
        high = (lane & step) != 0
        for i in range(16):
            if i & step:
                continue
            a, b = parts[i], parts[i + step]
            parts[i] = jnp.where(high, pltpu.roll(b, step, 1), a)
            parts[i + step] = jnp.where(high, b, pltpu.roll(a, LANES - step, 1))
    return parts


def pick(zone, table):
    for m in range(3):
        bit = (zone & (1 << m)) != 0
        table = [jnp.where(bit, table[i + 1], table[i]) for i in range(0, len(table), 2)]
    return table[0]


def kernel(
    sal_hbm, zone_hbm, flow_hbm, fixed_hbm, disp_ref, out_hbm,
    sal, zone, flow, fixed,
    long_nat, st, ft, ct, ys, yf, cy, yb, yc,
    us, uf, up, uq, ur,
    yd, yfd, yp, yw, yr, lev_a, lev_c, lev_i, tmp,
    gcoef, gval,
    sec, wu, pu, wd, pd, eu_in, ed_in, eu_out, ed_out, ru, rd, r_in, qu_out, qd_out, q_in, res,
    in_sem, s_send, s_recv, c_send, c_recv, f_send, f_recv, gc_send, gc_recv, gv_send, gv_recv,
    e_send, e_recv, r_send, r_recv, q_send, q_recv, out_sem,
):
    grp = lax.axis_index("grp")
    col = lax.axis_index("col")
    lay = lax.axis_index("lay")

    def partner(m):
        return ((col // 4 + (4 - m // 4) % 4) % 4) * 4 + (col % 4 + m % 4) % 4

    def s_copy(dest, source):
        return pltpu.make_async_remote_copy(
            src_ref=st.at[dest],
            dst_ref=ys.at[:, pl.ds(source * RB, RB), :],
            send_sem=s_send.at[dest],
            recv_sem=s_recv.at[source],
            device_id={"col": dest},
            device_id_type=MESH,
        )

    def f_copy(dest, source):
        return pltpu.make_async_remote_copy(
            src_ref=ft.at[dest],
            dst_ref=yf.at[:, pl.ds(source * RB, RB), :],
            send_sem=f_send.at[dest],
            recv_sem=f_recv.at[source],
            device_id={"col": dest},
            device_id_type=MESH,
        )

    def c_copy(dest, source):
        return pltpu.make_async_remote_copy(
            src_ref=ct.at[dest],
            dst_ref=cy.at[source],
            send_sem=c_send.at[dest],
            recv_sem=c_recv.at[source],
            device_id={"col": dest},
            device_id_type=MESH,
        )

    def g_copy(buf, send, recv, dest, source):
        return pltpu.make_async_remote_copy(
            src_ref=buf.at[source],
            dst_ref=buf.at[source],
            send_sem=send.at[dest],
            recv_sem=recv.at[source],
            device_id={"grp": dest},
            device_id_type=MESH,
        )

    def e_copy(way, c, dest):
        rows = pl.ds(pl.multiple_of(c * ZR, ZR), ZR)
        src, dst = ((eu_out, eu_in), (ed_out, ed_in))[way]
        return pltpu.make_async_remote_copy(
            src_ref=src.at[rows],
            dst_ref=dst.at[rows],
            send_sem=e_send.at[way, c],
            recv_sem=e_recv.at[way, c],
            device_id={"lay": dest},
            device_id_type=MESH,
        )

    def r_copy(way, dest):
        return pltpu.make_async_remote_copy(
            src_ref=(ru, rd)[way],
            dst_ref=r_in,
            send_sem=r_send.at[0],
            recv_sem=r_recv.at[0],
            device_id={"lay": dest},
            device_id_type=MESH,
        )

    def q_copy(way, c, dest, source):
        rows = pl.ds(pl.multiple_of(c * QR, QR), QR)
        return pltpu.make_async_remote_copy(
            src_ref=(qu_out, qd_out)[way].at[rows],
            dst_ref=q_in.at[source, rows],
            send_sem=q_send.at[c, dest],
            recv_sem=q_recv.at[c, source],
            device_id={"lay": dest},
            device_id_type=MESH,
        )

    def out_copy(c):
        rows = pl.ds(pl.multiple_of(c * QR, QR), QR)
        return pltpu.make_async_copy(res.at[:, rows, :], out_hbm.at[:, rows, :], out_sem.at[c])

    def ahead(way, k):
        return range(k + 1, NLAY) if way == 0 else range(k - 1, -1, -1)

    whole = (LINES, LANES)

    def to_steps(flat, steps_ref):
        for m in range(LINES // 8):
            for j in range(STEP):
                steps_ref[j, pl.ds(8 * m, 8), :] = flat[pl.ds(8 * STEP * m + j, 8, stride=STEP), :]

    def block_factors(steps_ref, w_ref, p_ref, r_ref):
        e = jnp.ones(whole, F32)
        r = jnp.ones(whole, F32)
        eb = jnp.ones(whole, F32)
        for j in range(1, STEP):
            s = steps_ref[j]
            se = s * e
            w = 1.0 / (1.0 + s + se)
            p = s * w
            e = (1.0 + se) * w
            r_now = r * p
            eb = eb - r * r_now
            r = r_now
            w_ref[j] = w
            p_ref[j] = p
            r_ref[j] = r
        return e, r, eb

    def e_stage(k):
        for way in range(2):

            @pl.when(lay == (k if way == 0 else NLAY - 1 - k))
            def _():
                me = k if way == 0 else NLAY - 1 - k
                src, out, wr, pr = ((eu_in, eu_out, wu, pu), (ed_in, ed_out, wd, pd))[way]

                def step(c, carry):
                    rows = pl.ds(pl.multiple_of(c * ZR, ZR), ZR)
                    if k > 0:
                        e_copy(way, c, me).wait_recv()
                        e = src[rows, :]
                    else:
                        e = jnp.ones((ZR, LANES), F32)
                    if k == NLAY - 1 and way == 1:
                        return carry
                    for i in range(L) if way == 0 else range(L - 1, -1, -1):
                        s = ys[i, rows, :]
                        se = s * e
                        w = 1.0 / (1.0 + s + se)
                        e = (1.0 + se) * w
                        p = s * w
                        wr[i, rows, :] = w
                        pr[i, rows, :] = p
                    if k < NLAY - 1:
                        out[rows, :] = e
                    if k < NLAY - 1:
                        e_copy(way, c, ahead(way, me)[0]).start()
                    return carry

                lax.fori_loop(0, ZCH, step, 0)

    loads = [
        pltpu.make_async_copy(zone_hbm, zone, in_sem.at[0]),
        pltpu.make_async_copy(flow_hbm, flow, in_sem.at[1]),
        pltpu.make_async_copy(fixed_hbm, fixed, in_sem.at[2]),
        pltpu.make_async_copy(sal_hbm, sal, in_sem.at[3]),
    ]
    for copy in loads:
        copy.start()

    barrier = pltpu.get_barrier_semaphore()

    def greet_col(o, carry):
        pl.semaphore_signal(barrier, inc=1, device_id={"col": (col + o) % NCOL}, device_id_type=MESH)
        return carry

    lax.fori_loop(1, NCOL, greet_col, 0)
    for o in range(1, NGRP):
        pl.semaphore_signal(barrier, inc=1, device_id={"grp": (grp + o) % NGRP}, device_id_type=MESH)
    for o in range(1, NLAY):
        pl.semaphore_signal(barrier, inc=1, device_id={"lay": (lay + o) % NLAY}, device_id_type=MESH)

    lane = lax.broadcasted_iota(jnp.int32, (8, LANES), 1)

    for copy in loads[:3]:
        copy.wait()
    table_long = [disp_ref[0, i] for i in range(8)]
    table_trans = [disp_ref[1, i] for i in range(8)]

    def couple(z, carry):
        for half in range(2):
            rows = pl.ds(8 * half, 8)
            for b in range(NCOL):
                cols = pl.ds(LANES * b, LANES)
                ids = zone[z, rows, cols]
                speed = flow[z, rows, cols]
                opened = 1.0 - fixed[z, rows, cols].astype(F32)
                st[b, z, rows, :] = opened * pick(ids, table_trans) * speed
                long_nat[b, z, rows, :] = opened * pick(ids, table_long) * speed
        return carry

    lax.fori_loop(0, L, couple, 0)

    pl.semaphore_wait(barrier, NCOL - 1 + NGRP - 1 + NLAY - 1)

    def s_start(o, carry):
        s_copy(partner(o), col).start()
        return carry

    lax.fori_loop(1, NCOL, s_start, 0)
    ys[:, pl.ds(col * RB, RB), :] = st[col]

    to_steps(st.reshape(NCOL * LINES, LANES), yd)
    block_factors(yd, yw, yp, yr)

    loads[3].wait()

    def spread(z, carry):
        for half in range(2):
            rows = pl.ds(8 * half, 8)
            line = pl.ds(pl.multiple_of(z * RB + 8 * half, 8), 8)
            s_parts = butterfly([long_nat[b, z, rows, :] for b in range(NCOL)], lane)
            for j in range(STEP):
                us[j, line, :] = s_parts[j]
            f_parts = butterfly([sal[z, rows, pl.ds(LANES * b, LANES)] for b in range(NCOL)], lane)
            for j in range(STEP):
                uf[j, line, :] = f_parts[j]
        return carry

    lax.fori_loop(0, L, spread, 0)

    e = jnp.ones(whole, F32)
    r = jnp.ones(whole, F32)
    q = jnp.zeros(whole, F32)
    alpha = jnp.zeros(whole, F32)
    eb = jnp.ones(whole, F32)
    for j in range(1, STEP):
        s = us[j]
        f = uf[j]
        se = s * e
        w = 1.0 / (1.0 + s + se)
        p = s * w
        e = (1.0 + se) * w
        q = f * w + p * q
        r_now = r * p
        alpha = alpha + r * q
        eb = eb - r * r_now
        r = r_now
        up[j] = p
        uq[j] = q
        ur[j] = r

    lanes = lax.broadcasted_iota(jnp.int32, whole, 1)
    sub = lanes // 16
    low = lanes % 16
    first_block = lanes == 0
    last_block = lanes == LANES - 1

    def before(v, d):
        if d >= 8:
            return pltpu.roll(v, d // 8, 1)
        return jnp.where(sub >= d, pltpu.roll(v, 16 * d, 1), pltpu.roll(v, 16 * d + 1, 1))

    def after(v, d):
        if d >= 8:
            return pltpu.roll(v, LANES - d // 8, 1)
        return jnp.where(
            sub < 8 - d, pltpu.roll(v, LANES - 16 * d, 1), pltpu.roll(v, LANES - 16 * d - 1, 1)
        )

    s = us[0]
    ep_left = jnp.where(first_block, 1.0, before(e, 1))
    q_left = jnp.where(first_block, 0.0, before(q, 1))
    r_left = jnp.where(first_block, 0.0, before(r, 1))
    inv = 1.0 / (1.0 + s * (eb + ep_left))
    a = s * r_left * inv
    c = jnp.where(last_block, 0.0, s * r * inv)
    f = (uf[0] + s * (q_left + alpha)) * inv
    for m in range(7):
        d = 1 << m
        inv = 1.0 / (1.0 - a * before(c, d) - c * after(a, d))
        f = (f + a * before(f, d) + c * after(f, d)) * inv
        if m < 6:
            a, c = a * before(a, d) * inv, c * after(c, d) * inv

    uf[0] = f
    x = jnp.where(last_block, 0.0, after(f, 1))
    for j in range(STEP - 1, 0, -1):
        x = uq[j] + ur[j] * f + up[j] * x
        uf[j] = x

    def gather(z, carry):
        for half in range(2):
            rows = pl.ds(8 * half, 8)
            line = pl.ds(pl.multiple_of(z * RB + 8 * half, 8), 8)
            parts = butterfly([uf[j, line, :] for j in range(STEP)], lane)
            for b in range(NCOL):
                ft[b, z, rows, :] = parts[b]
        return carry

    lax.fori_loop(0, L, gather, 0)

    ft_flat = ft.reshape(NCOL * LINES, LANES)
    to_steps(ft_flat, yfd)
    q = yfd[1] * yw[1]
    yfd[1] = q
    alpha = q
    for j in range(2, STEP):
        q = yfd[j] * yw[j] + yp[j] * q
        yfd[j] = q
        alpha = alpha + yr[j - 1] * q
    head = yfd[0] + yd[0] * alpha
    for b in range(NCOL):
        ct[b, 0:L] = head[L * b : L * (b + 1)]
        ct[b, L : 2 * L] = q[L * b : L * (b + 1)]

    def c_start(o, carry):
        c_copy(partner(o), col).start()
        return carry

    lax.fori_loop(1, NCOL, c_start, 0)
    cy[col] = ct[col]

    x = yfd[STEP - 1]
    for j in range(STEP - 1, -1, -1):
        if j == 0:
            x = jnp.zeros(whole, F32)
        elif j < STEP - 1:
            x = yfd[j] + yp[j] * x
        for m in range(LINES // 8):
            ft_flat[pl.ds(8 * STEP * m + j, 8, stride=STEP), :] = x[8 * m : 8 * m + 8]

    def f_start(o, carry):
        f_copy(partner(o), col).start()
        return carry

    lax.fori_loop(1, NCOL, f_start, 0)
    yf[:, pl.ds(col * RB, RB), :] = ft[col]

    def s_wait(o, carry):
        s_copy(col, (col + NCOL - o) % NCOL).wait_recv()
        return carry

    lax.fori_loop(1, NCOL, s_wait, 0)

    to_steps(ys.reshape(L * ROWS, LANES), yd)

    e, r, eb = block_factors(yd, yw, yp, yr)
    block = lax.broadcasted_iota(jnp.int32, whole, 0) % RB

    def above(v, d, edge):
        return jnp.where(block >= d, pltpu.roll(v, d, 0), edge)

    def below(v, d, edge):
        return jnp.where(block < RB - d, pltpu.roll(v, LINES - d, 0), edge)

    s = yd[0]
    inv = 1.0 / (1.0 + s * (eb + above(e, 1, 1.0)))
    a = s * above(r, 1, 1.0) * inv
    c = s * r * inv
    yw[0] = inv
    for m in range(4):
        d = 1 << m
        inv = 1.0 / (1.0 - a * above(c, d, 0.0) - c * below(a, d, 0.0))
        lev_a[m] = a * inv
        lev_c[m] = c * inv
        lev_i[m] = inv
        a, c = a * above(a, d, 1.0) * inv, c * below(c, d, 1.0) * inv
    lev_a[4] = a
    lev_c[4] = c
    top = pl.ds(0, L, stride=RB)
    bottom = pl.ds(RB - 1, L, stride=RB)
    tmp[0] = r * a
    tmp[1] = (1.0 - e) + r * c
    gcoef[grp, 0 * L : 1 * L] = lev_a[4, top, :]
    gcoef[grp, 1 * L : 2 * L] = lev_c[4, top, :]
    gcoef[grp, 2 * L : 3 * L] = tmp[0, bottom, :]
    gcoef[grp, 3 * L : 4 * L] = tmp[1, bottom, :]

    for o in range(1, NGRP):
        g_copy(gcoef, gc_send, gc_recv, (grp + o) % NGRP, grp).start()

    def c_wait(o, carry):
        c_copy(col, (col + NCOL - o) % NCOL).wait_recv()
        return carry

    lax.fori_loop(1, NCOL, c_wait, 0)
    for k in range(NCOL):
        tmp[2, pl.ds(k, L, stride=NCOL), :] = cy[k, 0:L]
        tmp[3, pl.ds(k, L, stride=NCOL), :] = cy[k, L : 2 * L]

    q = tmp[3]
    f = (tmp[2] + yd[0] * above(q, 1, 0.0)) * yw[0]
    for m in range(4):
        d = 1 << m
        f = f * lev_i[m] + lev_a[m] * above(f, d, 0.0) + lev_c[m] * below(f, d, 0.0)
    tmp[2] = f
    tmp[3] = q + yr[STEP - 1] * f
    gval[grp, 0 * L : 1 * L] = tmp[2, top, :]
    gval[grp, 1 * L : 2 * L] = tmp[3, bottom, :]

    for o in range(1, NGRP):
        g_copy(gval, gv_send, gv_recv, (grp + o) % NGRP, grp).start()

    e_stage(0)

    to_left = jnp.zeros(whole, F32)
    to_right = jnp.ones(whole, F32)
    yb_flat = yb.reshape(L * ROWS, LANES)
    yc_flat = yc.reshape(L * ROWS, LANES)
    for j in range(STEP - 1, -1, -1):
        if j == 0:
            to_left, to_right = jnp.ones(whole, F32), jnp.zeros(whole, F32)
        else:
            to_left = yr[j] + yp[j] * to_left
            to_right = yp[j] * to_right
        for m in range(LINES // 8):
            rows = pl.ds(8 * STEP * m + j, 8, stride=STEP)
            yb_flat[rows, :] = to_left[8 * m : 8 * m + 8]
            yc_flat[rows, :] = to_right[8 * m : 8 * m + 8]

    e_stage(1)

    for o in range(1, NGRP):
        g_copy(gcoef, gc_send, gc_recv, grp, (grp + NGRP - o) % NGRP).wait_recv()
    for o in range(1, NGRP):
        g_copy(gval, gv_send, gv_recv, grp, (grp + NGRP - o) % NGRP).wait_recv()

    be = [gcoef[g, 0 * L : 1 * L] for g in range(NGRP)]
    ga = [gcoef[g, 1 * L : 2 * L] for g in range(NGRP)]
    rr = [gcoef[g, 2 * L : 3 * L] for g in range(NGRP)]
    pp = [gcoef[g, 3 * L : 4 * L] for g in range(NGRP)]
    al = [gval[g, 0 * L : 1 * L] for g in range(NGRP)]
    qq = [gval[g, 1 * L : 2 * L] for g in range(NGRP)]
    pre_p, pre_q = [pp[0]], [qq[0]]
    for g in range(1, NGRP - 1):
        t = rr[g] / (1.0 - pre_p[-1] * be[g])
        pre_p, pre_q = (
            pre_p + [pp[g] + t * pre_p[-1] * ga[g]],
            pre_q + [qq[g] + t * (pre_q[-1] + pre_p[-1] * al[g])],
        )
    suf_p, suf_q = [be[NGRP - 1]], [al[NGRP - 1]]
    for g in range(NGRP - 2, 0, -1):
        t = ga[g] * suf_p[0] / (1.0 - pp[g] * suf_p[0])
        suf_p, suf_q = (
            [be[g] + t * rr[g]] + suf_p,
            [al[g] + ga[g] * suf_q[0] + t * (qq[g] + pp[g] * suf_q[0])] + suf_q,
        )
    left = jnp.zeros((L, LANES), F32)
    right = jnp.zeros((L, LANES), F32)
    for i in range(NGRP - 1):
        u = (pre_q[i] + pre_p[i] * suf_q[i]) / (1.0 - pre_p[i] * suf_p[i])
        v = suf_q[i] + suf_p[i] * u
        left = jnp.where(grp == i + 1, u, left)
        right = jnp.where(grp == i, v, right)

    def per_line(v):
        return jnp.concatenate([jnp.broadcast_to(v[z : z + 1], (RB, LANES)) for z in range(L)], 0)

    right = per_line(right)
    f = f + lev_a[4] * per_line(left) + lev_c[4] * right
    tmp[2] = f
    tmp[3] = jnp.where(block == RB - 1, right, pltpu.roll(f, LINES - 1, 0))


    def fill(c):
        for n in range(QR // RB):
            source = c * (QR // RB) + n

            @pl.when(source != col)
            def _():
                f_copy(col, source).wait_recv()

        for z in range(L):
            for n in range(QR // RB):
                rows = pl.ds(pl.multiple_of(c * QR + RB * n, RB), RB)
                line = pl.ds(z * NCOL + c * (QR // RB) + n, 1)
                sec[z, rows, :] = yf[z, rows, :] + yb[z, rows, :] * tmp[2, line, :] + yc[z, rows, :] * tmp[3, line, :]

    def q_pass(k, way, back):
        out, wr, pr = ((qu_out, wu, pu), (qd_out, wd, pd))[way]
        order = list(range(L) if way == 0 else range(L - 1, -1, -1))
        behind = k - 1 if way == 0 else k + 1

        def step(i, carry):
            c = (i + col // 4) % QCH
            rows = pl.ds(pl.multiple_of(c * QR, QR), QR)
            if back < 2:
                fill(c)
            if back > 0:
                q_copy(0, c, k, behind).wait_recv()
                q = q_in[behind, rows, :]
            for i in order:
                mine = sec[i, rows, :] * wr[i, rows, :]
                q = mine if (back == 0 and i == order[0]) else mine + pr[i, rows, :] * q
            out[rows, :] = q
            q_copy(way, c, ahead(way, k)[0], k).start()
            return carry

        lax.fori_loop(0, QCH, step, 0)

    for k, way, back in ((0, 0, 0), (1, 0, 1), (2, 1, 1), (3, 1, 0)):

        @pl.when(lay == k)
        def _():
            q_pass(k, way, back)

    e_stage(2)
    for k, way in ((1, 1), (2, 0)):

        @pl.when(lay == k)
        def _():
            q_pass(k, way, 2)

    e_stage(3)

    for k in range(NLAY):

        @pl.when(lay == k)
        def _():
            below_from = {0: None, 1: 0, 2: 1, 3: 2}[k]
            above_from = {0: 1, 1: 2, 2: 3, 3: None}[k]

            def finish(i, carry):
                c = (i + col // 4) % QCH
                rows = pl.ds(pl.multiple_of(c * QR, QR), QR)
                if k in (0, NLAY - 1):
                    q_copy(0, c, k, 1 if k == 0 else 2).wait_recv()
                q = None if below_from is None else q_in[below_from, rows, :]
                q_all = []
                for i in range(L):
                    mine = sec[i, rows, :] * wu[i, rows, :]
                    q = mine if q is None else mine + pu[i, rows, :] * q
                    q_all.append(q)
                x = q
                if above_from is not None:
                    ep = eu_out[rows, :]
                    p = 1.0 - ep
                    x = (q + p * q_in[above_from, rows, :]) / (ep + p * ed_in[rows, :])
                out_hbm[L - 1, rows, :] = x
                for i in range(L - 2, -1, -1):
                    x = q_all[i] + pu[i, rows, :] * x
                    out_hbm[i, rows, :] = x
                return carry

            lax.fori_loop(0, QCH, finish, 0)

    def s_done(o, carry):
        s_copy((col + o) % NCOL, col).wait_send()
        c_copy((col + o) % NCOL, col).wait_send()
        f_copy((col + o) % NCOL, col).wait_send()
        return carry

    lax.fori_loop(1, NCOL, s_done, 0)
    for o in range(1, NGRP):
        g_copy(gcoef, gc_send, gc_recv, (grp + o) % NGRP, grp).wait_send()
        g_copy(gval, gv_send, gv_recv, (grp + o) % NGRP, grp).wait_send()
    for k in range(NLAY):

        @pl.when(lay == k)
        def _():
            for way in range(2):
                back = k if way == 0 else NLAY - 1 - k
                if back == NLAY - 1:
                    continue
                dest = ahead(way, k)[0]
                for c in range(ZCH):
                    e_copy(way, c, dest).wait_send()
                for c in range(QCH):
                    q_copy(way, c, dest, k).wait_send()


def per_device(salinity, zone_ids, flow_speed, fixed_cells, dispersivity):
    hbm = pl.BlockSpec(memory_space=pl.ANY)
    fixed = pl.BlockSpec(memory_space=pltpu.HBM)
    nat = (L, RB, NCOL * LANES)
    slab = (L, ROWS, LANES)
    by_dest = (NCOL, L, RB, LANES)
    steps = (STEP, LINES, LANES)
    plane = (ROWS, LANES)

    def vm(shape, dtype=F32):
        return pltpu.VMEM(shape, dtype)

    dma = pltpu.SemaphoreType.DMA
    return pl.pallas_call(
        kernel,
        out_shape=jax.ShapeDtypeStruct(slab, F32),
        in_specs=[hbm, hbm, hbm, hbm, pl.BlockSpec(memory_space=pltpu.SMEM)],
        out_specs=pl.BlockSpec(memory_space=pltpu.VMEM),
        scratch_shapes=[
            vm(nat), vm(nat, jnp.int32), vm(nat), vm(nat, jnp.int32),
            vm(by_dest), vm(by_dest), vm(by_dest), vm((NCOL, 2 * L, LANES)), vm(slab), vm(slab),
            vm((NCOL, 2 * L, LANES)), vm(slab), vm(slab),
            vm(steps), vm(steps), vm(steps), vm(steps), vm(steps),
            vm(steps), vm(steps), vm(steps), vm(steps), vm(steps),
            vm((5, LINES, LANES)), vm((5, LINES, LANES)), vm((4, LINES, LANES)), vm((4, LINES, LANES)),
            vm((NGRP, 4 * L, LANES)), vm((NGRP, 2 * L, LANES)),
            vm(slab), vm(slab), vm(slab), vm(slab), vm(slab),
            vm(plane), vm(plane), vm(plane), vm(plane), vm(plane), vm(plane), vm(plane),
            vm(plane), vm(plane), vm((NLAY,) + plane), vm(slab),
            dma((4,)), dma((NCOL,)), dma((NCOL,)), dma((NCOL,)), dma((NCOL,)), dma((NCOL,)), dma((NCOL,)),
            dma((NGRP,)), dma((NGRP,)), dma((NGRP,)), dma((NGRP,)),
            dma((2, ZCH)), dma((2, ZCH)), dma((1,)), dma((1,)), dma((QCH, NLAY)), dma((QCH, NLAY)), dma((QCH,)),
        ],
        compiler_params=pltpu.CompilerParams(
            collective_id=0, has_side_effects=True, vmem_limit_bytes=54272 * 1024
        ),
        name="lod_step",
    )(salinity, zone_ids, flow_speed, fixed_cells, dispersivity)


def solution(mesh):
    placed = P("lay", ("grp", "col"), None)
    return jax.shard_map(
        per_device,
        mesh=mesh,
        in_specs=(placed, placed, placed, placed, P()),
        out_specs=P("lay", "grp", "col"),
        check_vma=False,
    )
```
